128 devices in a mesh: wall: 8 (over y, core), cell: 16 (over x, z).
Axes of the slice: x: 4, y: 4, z: 4, core: 2. Of those that a mesh axis runs over, the one named last changes fastest.
Arguments:
- cell_points: float32 [256, 3, 544], P(('wall', 'cell')), may hold values from -4 to 64, as said below
- cell_force: float32 [256, 3, 544], P(('wall', 'cell')), may hold values from -120 to 120
- cell_weight: float32 [256, 544], P(('wall', 'cell')), may hold values from 0.01 to 0.05
- partners: int32 [256, 8], P(('wall', 'cell')), may hold values from -1 to 31, as said below
- wall_points: float32 [3, 98304], P(None, ('wall', 'cell')), may hold values from -4 to 64, as said below
- wall_area: float32 [98304], P(('wall', 'cell')), may hold values from 0.01 to 0.04
- wall_data: float32 [3, 98304], P(None, ('wall', 'cell')), may hold values from -30 to 30
Outputs:
- cell_velocity: float32 [256, 3, 544], P(('wall', 'cell'))
- wall_density: float32 [3, 98304], P(None, ('wall', 'cell'))
The draws below stay inside these ranges and needn't reach their ends.
Inputs may be any that keep to these rules, and one draw needn't show every extreme that they name: `partners`: cell numbers within the segment or -1. Cell n of a segment is held by device n // 2 of that segment. No cell names itself. Among the rows of one device, at most 2 entries name cells of any one device, and some device is named exactly 2 times there. `cell_points`: points of closed surfaces of radius about one inside the vessel of segment s, which runs from 8 s to 8 s + 8 along the first coordinate. `wall_points`: points on the vessel wall of radius 4 about the first coordinate axis; the points of segment s lie between 8 s and 8 s + 8 along it.
All inputs are finite; a program needn't handle non-finite values.
Results may differ from the reference program's by a relative error of at most 0.0003.
Values sent between devices are 32-bit elements; how exact they have to be, the bound alone decides.
No kernel may reach another device: no remote copies, remote signals or barrier semaphores. Data moves between devices by JAX's collectives and lax.ppermute only.
A program may use at most 64 MiB of HBM per device.

```python
import math
import jax
import jax.numpy as jnp
from jax import lax

Q = 544
KP = 8
ITERS = 4
CELL_DEV = 2
WPD = 768
CAP = 2
CELLS_GROUP = 32
CELLS = 256
WALL_GROUP = 12288
WALL_PTS = 98304
N_WALL = 8


def draw_cell_points(key, part):
    keys = jax.random.split(key, 5)
    index = jnp.arange(CELLS, dtype=jnp.int32)
    segment = (index // CELLS_GROUP).astype(jnp.float32)
    along = (segment + jax.random.uniform(keys[0], (CELLS,), jnp.float32, 0.16, 0.84)) * 8.0
    radial = 2.4 * jnp.sqrt(jax.random.uniform(keys[1], (CELLS,), jnp.float32))
    turn = jax.random.uniform(keys[2], (CELLS,), jnp.float32, -math.pi, math.pi)
    centers = jnp.stack([along, radial * jnp.cos(turn), radial * jnp.sin(turn)], axis=1)
    raw = jax.random.normal(keys[3], (CELLS, 3, Q), jnp.float32)
    length = jnp.sqrt(jnp.sum(raw * raw, axis=1, keepdims=True))
    direction = raw / jnp.maximum(length, 0.3)
    radius = jnp.clip(1.0 + 0.08 * jax.random.normal(keys[4], (CELLS, 1, Q), jnp.float32), 0.8, 1.2)
    return centers[:, :, None] + direction * radius


def draw_wall_points(key, part):
    keys = jax.random.split(key, 2)
    index = jnp.arange(WALL_PTS, dtype=jnp.int32)
    segment = (index // WALL_GROUP).astype(jnp.float32)
    along = (segment + jax.random.uniform(keys[0], (WALL_PTS,), jnp.float32)) * 8.0
    turn = jax.random.uniform(keys[1], (WALL_PTS,), jnp.float32, -math.pi, math.pi)
    return jnp.stack([along, 4.0 * jnp.cos(turn), 4.0 * jnp.sin(turn)], axis=0)


def draw_wall_data(key, part):
    keys = jax.random.split(key, 2)
    position = jnp.arange(WALL_PTS, dtype=jnp.float32)
    rising = 1.0 + 2.0 * position / WALL_PTS
    spread = jnp.exp(jax.random.uniform(keys[0], (1, WALL_PTS), jnp.float32, -1.15, 1.15))
    base_vals = jax.random.normal(keys[1], (3, WALL_PTS), jnp.float32)
    return jnp.clip(0.5 * base_vals * spread * rising[None, :], -30.0, 30.0)


def draw_partners(key, part):
    keys = jax.random.split(key, 5)
    devices = CELLS // CELL_DEV
    entries = CELL_DEV * KP
    peers = CELLS_GROUP // CELL_DEV
    orders = jax.vmap(lambda sub: jax.random.permutation(sub, peers))(jax.random.split(keys[0], devices))
    block_of = jnp.arange(entries, dtype=jnp.int32) // CAP
    owner = orders[:, block_of]
    level = jax.random.randint(keys[1], (devices, 1), 0, 6)
    rolled = jax.random.randint(keys[2], (devices, entries), 0, 12)
    keep = jnp.logical_or(rolled >= level, block_of[None, :] == 0)
    shuffles = jax.vmap(lambda sub: jax.random.permutation(sub, entries))(jax.random.split(keys[3], devices))
    owner = jnp.take_along_axis(owner, shuffles, axis=1)
    keep = jnp.take_along_axis(keep, shuffles, axis=1)
    within = jax.random.randint(keys[4], (devices, entries), 0, CELL_DEV)
    local_device = (jnp.arange(devices, dtype=jnp.int32) % peers)[:, None]
    requester = local_device * CELL_DEV + jnp.arange(entries, dtype=jnp.int32)[None, :] // KP
    chosen = owner * CELL_DEV + within
    chosen = jnp.where(chosen == requester, owner * CELL_DEV + (within + 1) % CELL_DEV, chosen)
    result = jnp.where(keep, chosen, -1)
    return result.reshape(CELLS, KP).astype(jnp.int32)


def level_of(own_key, dims, cuts, smallest, largest):
    factor_of, own = 1.0, jax.random.fold_in(own_key, 6)
    for axis_at, shards_of in cuts:
        heights = jnp.exp(jax.random.uniform(jax.random.fold_in(own, axis_at), (shards_of,), jnp.float32, smallest / len(cuts), largest / len(cuts)))
        factor_of = factor_of * jnp.repeat(heights, dims[axis_at] // shards_of).reshape([-1 if axis == axis_at else 1 for axis in range(len(dims))])
    return factor_of


def centred(own_key, extent, deviation, limit, cuts=(), kind=jnp.bfloat16):
    gain = level_of(own_key, extent, cuts, -0.22, 0.18) if cuts else 1.0
    values = jax.random.normal(own_key, extent, jnp.float32) * deviation * gain
    return jnp.minimum(jnp.maximum(values, -limit), limit).astype(kind)


def setup_inputs(seed: int = 0) -> dict:
    key_list = jax.random.split(jax.random.key(seed), 8)
    return {
        "cell_points": draw_cell_points(jax.random.fold_in(key_list[7], 71), 0),
        "cell_force": centred(key_list[1], (CELLS, 3, Q), 20.0, 120.0, ((0, 128),), jnp.float32),
        "cell_weight": jnp.clip(jnp.exp(math.log(0.05) - 1.609438 * jax.random.uniform(key_list[2], (CELLS, Q), jnp.float32) ** level_of(key_list[2], (CELLS, Q), ((0, 128),), -0.2, 0.2)), 0.01, 0.05),
        "partners": draw_partners(jax.random.fold_in(key_list[7], 71), 0),
        "wall_points": draw_wall_points(jax.random.fold_in(key_list[7], 71), 0),
        "wall_area": jnp.clip(jnp.exp(math.log(0.04) - 1.3862944 * jax.random.uniform(key_list[5], (WALL_PTS,), jnp.float32) ** level_of(key_list[5], (WALL_PTS,), ((0, 128),), -0.2, 0.2)), 0.01, 0.04),
        "wall_data": draw_wall_data(jax.random.fold_in(key_list[7], 71), 0),
    }


blob_width = 0.1
norm_floor = 1e-06

def stokeslet(targets, sources, strength):
    offsets = targets[:, :, None] - sources[:, None, :]
    square_dist = lax.optimization_barrier(jnp.sum(offsets * offsets, axis=0))
    shifted = square_dist + blob_width * blob_width
    factor = 1.0 / (8.0 * math.pi * shifted * jnp.sqrt(shifted))
    projected = lax.optimization_barrier(jnp.sum(strength[:, None, :] * offsets, axis=0))
    terms = (square_dist + 2.0 * blob_width * blob_width)[None] * strength[:, None, :] + projected[None] * offsets
    return lax.optimization_barrier(jnp.sum(factor[None] * terms, axis=2))

def field_blocks(targets, sources, strength, block):
    count = sources.shape[1] // block
    source_blocks = jnp.transpose(sources.reshape(3, count, block), (1, 0, 2))
    strength_blocks = jnp.transpose(strength.reshape(3, count, block), (1, 0, 2))

    def add_block(carry, pieces):
        return (carry + stokeslet(targets, pieces[0], pieces[1]), None)
    total, unused = lax.scan(add_block, jnp.zeros(targets.shape, jnp.float32), (source_blocks, strength_blocks))
    return total

def near_cell(own_points, own_strength, more_points, more_strength):
    all_points = jnp.concatenate([own_points[None], more_points], axis=0)
    all_strength = jnp.concatenate([own_strength[None], more_strength], axis=0)

    def add_source(carry, pieces):
        return (carry + stokeslet(own_points, pieces[0], pieces[1]), None)
    total, unused = lax.scan(add_source, jnp.zeros(own_points.shape, jnp.float32), (all_points, all_strength))
    return total

def solve_small(hess, beta):
    size = len(hess[0])
    upper = [[hess[row][column] for column in range(size)] for row in range(size + 1)]
    targets = [beta] + [jnp.zeros((), jnp.float32) for column in range(size)]
    cosines = []
    sines = []
    for column in range(size):
        for prior in range(column):
            first_val = upper[prior][column]
            second_val = upper[prior + 1][column]
            upper[prior][column] = cosines[prior] * first_val + sines[prior] * second_val
            upper[prior + 1][column] = -sines[prior] * first_val + cosines[prior] * second_val
        first_val = upper[column][column]
        second_val = upper[column + 1][column]
        radius = jnp.sqrt(first_val * first_val + second_val * second_val)
        cosines.append(first_val / radius)
        sines.append(second_val / radius)
        upper[column][column] = radius
        targets[column + 1] = -sines[column] * targets[column]
        targets[column] = cosines[column] * targets[column]
    weights = [None for column in range(size)]
    for column in reversed(range(size)):
        partial_val = targets[column]
        for later in range(column + 1, size):
            partial_val = partial_val - upper[column][later] * weights[later]
        weights[column] = partial_val / upper[column][column]
    return weights

def reference(cell_points, cell_force, cell_weight, partners, wall_points, wall_area, wall_data):
    strength = cell_force * cell_weight[:, None, :]
    index = jnp.arange(CELLS, dtype=jnp.int32)
    base = index // CELLS_GROUP * CELLS_GROUP
    valid = partners >= 0
    rows = jnp.where(valid, base[:, None] + partners, 0).astype(jnp.int32)

    def one_cell(pieces):
        own_points, own_strength, row_ids, row_valid = pieces
        more_points = cell_points[row_ids]
        more_strength = strength[row_ids] * row_valid[:, None, None].astype(jnp.float32)
        return near_cell(own_points, own_strength, more_points, more_strength)
    near = lax.map(one_cell, (cell_points, strength, rows, valid))
    grouped_points = jnp.transpose(wall_points.reshape(3, N_WALL, WALL_GROUP), (1, 0, 2))

    def wall_apply(vector):
        source_strength = vector * wall_area[None, :]
        grouped_strength = jnp.transpose(source_strength.reshape(3, N_WALL, WALL_GROUP), (1, 0, 2))

        def one_group(pieces):
            group_points, group_strength = pieces
            target_blocks = jnp.transpose(group_points.reshape(3, WALL_GROUP // WPD, WPD), (1, 0, 2))
            fields = lax.map(lambda target: field_blocks(target, group_points, group_strength, WPD), target_blocks)
            return jnp.transpose(fields, (1, 0, 2)).reshape(3, WALL_GROUP)
        field = lax.map(one_group, (grouped_points, grouped_strength))
        return 0.5 * vector + jnp.transpose(field, (1, 0, 2)).reshape(3, WALL_PTS)
    beta = jnp.sqrt(jnp.sum(wall_data * wall_data) + norm_floor)
    basis = [wall_data / beta]
    zero_val = jnp.zeros((), jnp.float32)
    hess = [[zero_val for column in range(ITERS)] for row in range(ITERS + 1)]
    for column in range(ITERS):
        work = wall_apply(basis[column])
        for row in range(column + 1):
            coeff = jnp.sum(work * basis[row])
            hess[row][column] = coeff
            work = work - coeff * basis[row]
        scale_val = jnp.sqrt(jnp.sum(work * work) + norm_floor)
        hess[column + 1][column] = scale_val
        basis.append(work / scale_val)
    weights = solve_small(hess, beta)
    density = weights[0] * basis[0]
    for column in range(1, ITERS):
        density = density + weights[column] * basis[column]
    density_strength = density * wall_area[None, :]
    grouped_density = jnp.transpose(density_strength.reshape(3, N_WALL, WALL_GROUP), (1, 0, 2))
    grouped_cells = cell_points.reshape(N_WALL, CELLS_GROUP, 3, Q)

    def cells_group(pieces):
        group_points, group_strength, cells = pieces
        return lax.map(lambda target: field_blocks(target, group_points, group_strength, WPD), cells)
    wall_part = lax.map(cells_group, (grouped_points, grouped_density, grouped_cells)).reshape(CELLS, 3, Q)
    return (near + wall_part, density)
```

```python
import math

import jax
import jax.numpy as jnp
from jax import lax
from jax.experimental import pallas as pl
from jax.experimental.pallas import tpu as pltpu
from jax.sharding import PartitionSpec as P

F32 = jnp.float32
BF16 = jnp.bfloat16
AXES = ("wall", "cell")
E2 = 0.1 * 0.1
FLOOR = 1e-06
SCALE = 1.0 / (8.0 * math.pi)
VMEM_LIMIT = 48 * 2**20


def row_of(n):
    return lax.broadcasted_iota(jnp.int32, (8, n), 0)


def split3(a):
    high = a.astype(BF16).astype(F32)
    rest = a - high
    mid = rest.astype(BF16).astype(F32)
    low = (rest - mid).astype(BF16).astype(F32)
    return high, mid, low


def target_rows(points):
    n = points.shape[1]
    row = row_of(n)
    coords = jnp.where(row < 3, points, 0.0)
    norm2 = jnp.sum(coords * coords, axis=0, keepdims=True) + E2
    eight = jnp.where(row < 3, -2.0 * coords, jnp.where(row == 3, 1.0, jnp.where(row == 4, norm2, 0.0)))
    h, m, l = split3(eight)
    wide = jnp.concatenate([h, m, l, h, m, h] + [jnp.zeros_like(h)] * 10, axis=0)
    return jnp.transpose(wide)[:, :48].astype(BF16)


def source_columns(points):
    n = points.shape[1]
    row = row_of(n)
    coords = jnp.where(row < 3, points, 0.0)
    norm2 = jnp.sum(coords * coords, axis=0, keepdims=True)
    eight = jnp.where(row < 3, coords, jnp.where(row == 3, norm2, jnp.where(row == 4, 1.0, 0.0)))
    h, m, l = split3(eight)
    return jnp.concatenate([h, h, h, m, m, l], axis=0).astype(BF16)


def moment_rows(points, twice):
    n = points.shape[1]
    row = row_of(n)
    coords = jnp.where(row < 3, points, 0.0)
    y0, y1, y2 = points[0:1], points[1:2], points[2:3]
    norm2 = jnp.sum(coords * coords, axis=0, keepdims=True)
    inner = jnp.sum(coords * twice, axis=0, keepdims=True)
    first = twice * jnp.where(row < 4, 1.0, y0)
    second = twice * jnp.where(row < 4, y1, y2)
    third = jnp.where(row < 4, norm2 * twice + inner * coords, 0.0)
    return first, second, third


def moment_block(blocks):
    parts = [split3(b) for b in blocks]
    rows = [p[k] for k in range(3) for p in parts]
    return jnp.concatenate(rows, axis=0).astype(BF16)


def accumulate(acc, left, right, moments, blocks, hilo):
    dims = (((1,), (1,)), ((), ()))
    for start, size in blocks:
        shifted = jnp.dot(left[start : start + size, :], right, preferred_element_type=F32)
        inv = lax.rsqrt(shifted)
        kern = inv * inv * inv
        high = kern.astype(BF16)
        term = lax.dot_general(high, moments, dims, preferred_element_type=F32)
        if hilo:
            low = (kern - high.astype(F32)).astype(BF16)
            term = term + lax.dot_general(low, moments, dims, preferred_element_type=F32)
        acc[start : start + size, : term.shape[1]] += term


def assemble(points, f, t0, t1, t2, e):
    n = points.shape[1]
    row = lax.broadcasted_iota(jnp.int32, (4, n), 0)
    x4 = jnp.where(row < 3, points[0:4], 0.0)
    x0, x1, x2 = x4[0:1], x4[1:2], x4[2:3]
    norm2 = jnp.sum(x4 * x4, axis=0, keepdims=True)
    along = jnp.sum(x4 * f, axis=0, keepdims=True) - (t0[0:1] + t1[1:2] + t2[2:3])
    s0 = jnp.sum(x4 * t0, axis=0, keepdims=True)
    s1 = jnp.sum(x4 * t1, axis=0, keepdims=True)
    s2 = jnp.sum(x4 * t2, axis=0, keepdims=True)
    cross = jnp.where(row == 0, s0, jnp.where(row == 1, s1, jnp.where(row == 2, s2, 0.0)))
    return (norm2 + 2.0 * E2) * f + e - 2.0 * (x0 * t0 + x1 * t1 + x2 * t2) + x4 * along - cross


def velocity(points, acc):
    rows = jnp.transpose(acc)
    rows = rows[0:24] + rows[24:48] + rows[48:72]
    return assemble(points, rows[0:4], rows[4:8], rows[8:12], rows[12:16], rows[16:20])


def scalars(reds):
    first = reds[0]
    beta2 = first[0] + FLOOR
    beta = jnp.sqrt(beta2)
    g = {(0, 0): first[0] / beta2}
    hess = {}
    comb = []
    for j in range(len(reds)):
        if j == 0:
            b, ss = [first[1] / beta2], first[2] / beta2
        else:
            b, ss = reds[j][:-1], reds[j][-1]
        gram = lambda p, q: g[(min(p, q), max(p, q))]
        c = []
        for i in range(j + 1):
            h = 0.5 * gram(i, j) + b[i]
            for k in range(i):
                h = h - hess[(k, j)] * gram(k, i)
            hess[(i, j)] = h
            c.append(h - 0.5 if i == j else h)
        norm2 = ss
        for i in range(j + 1):
            norm2 = norm2 - 2.0 * c[i] * b[i]
            for k in range(j + 1):
                norm2 = norm2 + c[i] * c[k] * gram(i, k)
        norm2 = jnp.maximum(norm2, 0.0)
        h = jnp.sqrt(norm2 + FLOOR)
        hess[(j + 1, j)] = h
        for i in range(j + 1):
            v = b[i]
            for k in range(j + 1):
                v = v - c[k] * gram(i, k)
            g[(i, j + 1)] = v / h
        g[(j + 1, j + 1)] = norm2 / (h * h)
        comb.append((c, h))
    return beta, hess, comb


def solve_small(hess, beta, size):
    zero = jnp.zeros_like(beta)
    upper = [[hess.get((r, c), zero) for c in range(size)] for r in range(size + 1)]
    targets = [beta] + [zero] * size
    cosines, sines = [], []
    for column in range(size):
        for prior in range(column):
            a, b = upper[prior][column], upper[prior + 1][column]
            upper[prior][column] = cosines[prior] * a + sines[prior] * b
            upper[prior + 1][column] = cosines[prior] * b - sines[prior] * a
        a, b = upper[column][column], upper[column + 1][column]
        radius = jnp.sqrt(a * a + b * b)
        cosines.append(a / radius)
        sines.append(b / radius)
        upper[column][column] = radius
        targets[column + 1] = -sines[column] * targets[column]
        targets[column] = cosines[column] * targets[column]
    weights = [None] * size
    for column in reversed(range(size)):
        part = targets[column]
        for later in range(column + 1, size):
            part = part - upper[column][later] * weights[later]
        weights[column] = part / upper[column][column]
    return weights


def red_rows(ref, count):
    total = jnp.sum(ref[...], axis=0)
    return [total[k : k + 1, 0:1] for k in range(count)]


def put_sums(out, values):
    row = lax.broadcasted_iota(jnp.int32, (8, 128), 0)
    tile = jnp.zeros((8, 128), F32)
    for k, v in enumerate(values):
        tile = jnp.where(row == k, jnp.broadcast_to(v, (8, 128)), tile)
    for p in range(out.shape[0]):
        out[p] = tile


def total(a):
    while a.ndim > 2:
        a = jnp.sum(a, axis=0)
    return jnp.sum(jnp.sum(a, axis=0, keepdims=True), axis=1, keepdims=True)


def call(body, outs, ins, name, scratch=(), smem=()):
    specs = [pl.BlockSpec(memory_space=pltpu.SMEM if k in smem else pltpu.VMEM) for k in range(len(ins))]
    many = isinstance(outs, (list, tuple))
    ospec = pl.BlockSpec(memory_space=pltpu.VMEM)
    return pl.pallas_call(
        body,
        out_shape=outs,
        in_specs=specs,
        out_specs=[ospec] * len(outs) if many else ospec,
        scratch_shapes=list(scratch),
        compiler_params=pltpu.CompilerParams(vmem_limit_bytes=VMEM_LIMIT),
        name=name,
    )(*ins)


def shape(*dims, dtype=F32):
    return jax.ShapeDtypeStruct(dims, dtype)


def blocks_of(n, size):
    return [(k * size, size) for k in range(n // size)]


def near_body(partners, own, everyone, out, left, acc, sources):
    cells = own.shape[0]
    width = own.shape[2]
    slots = partners.shape[1]
    used = out.shape[2]
    row = row_of(width)

    def one(i, _):
        mine = own[i]
        centre = jnp.where(row < 3, mine[:, 0:1], 0.0)
        sources[:, 0:width] = mine - centre
        for k in range(slots):
            n = partners[i, k]
            there = jnp.maximum(n, 0)
            other = everyone[there // cells, there % cells] - centre
            keep = jnp.where(n >= 0, 1.0, 0.0)
            sources[:, (k + 1) * width : (k + 2) * width] = jnp.where(row >= 4, other * keep, other)
        sources[:, (slots + 1) * width :] = jnp.zeros((8, width), F32)
        left[...] = target_rows(mine - centre)
        acc[...] = jnp.zeros_like(acc)

        def step(s, _):
            pts = sources[:, pl.ds(pl.multiple_of(s * 2 * width, 2 * width), 2 * width)]
            r = row_of(2 * width)
            twice = SCALE * jnp.where(r >= 4, pts, pltpu.roll(pts, 4, 0))
            moments = moment_block(moment_rows(pts, twice))
            accumulate(acc, left, source_columns(pts), moments, blocks_of(used, used // 2), True)
            return 0

        lax.fori_loop(0, (slots + 2) // 2, step, 0)
        vel = velocity(mine - centre, acc[...])
        out[i] = vel[0:3, :used]
        return 0

    lax.fori_loop(0, cells, one, 0)


def first_body(mine, group, right, out, left, acc):
    n = mine.shape[1]
    left[...] = target_rows(mine[...])
    acc[...] = jnp.zeros_like(acc)
    row = row_of(n)

    def step(s, _):
        pts = group[s]
        cols = source_columns(pts)
        right[s] = cols
        area = SCALE * pts[3:4]
        twice = area * jnp.where(row >= 4, pts, pltpu.roll(pts, 4, 0))
        moments = moment_block(moment_rows(pts, twice))
        accumulate(acc, left, cols, moments, blocks_of(n, 256), HILO)
        return 0

    lax.fori_loop(0, group.shape[0], step, 0)
    vel = velocity(mine[...], acc[...])
    for p in range(out.shape[0]):
        out[p] = vel


def apply_body(mine, group, right, vector, out, left, acc):
    n = mine.shape[1]
    left[...] = target_rows(mine[...])
    acc[...] = jnp.zeros_like(acc)

    def step(s, _):
        pts = group[s]
        four = vector[s] * (SCALE * pts[3:4])
        moments = moment_block(moment_rows(pts, jnp.concatenate([four, four], axis=0)))
        accumulate(acc, left, right[s], moments, blocks_of(n, 256), HILO)
        return 0

    lax.fori_loop(0, group.shape[0], step, 0)
    out[...] = velocity(mine[...], acc[...])


def data_rows(block):
    return block[:, 4:8, :]


def pre1_body(group, u0, out):
    d = data_rows(group[...])
    u = u0[...]
    put_sums(out, [total(d * d), total(u * d), total(u * u)])


def pre2_body(red1, group, u0, s1, v1, out):
    beta, _, comb = scalars([red_rows(red1, 3)])
    (c,), h = comb[0]
    v0 = data_rows(group[...]) / beta
    one = (u0[...] / beta - c * v0) / h
    v1[...] = one
    s = s1[...]
    put_sums(out, [total(s * v0), total(s * one), total(s * s)])


def pre3_body(red1, red2, group, v1, s1, s2, v2, out):
    beta, _, comb = scalars([red_rows(red1, 3), red_rows(red2, 3)])
    (c0, c1), h = comb[1]
    v0 = data_rows(group[...]) / beta
    one = v1[...]
    two = (s1[...] - c0 * v0 - c1 * one) / h
    v2[...] = two
    s = s2[...]
    put_sums(out, [total(s * v0), total(s * one), total(s * two), total(s * s)])


def post1_body(red1, u0, t1, out):
    beta, _, comb = scalars([red_rows(red1, 3)])
    (c,), h = comb[0]
    s0 = u0[0] / beta
    s1 = (t1[...] / beta - c * s0) / h
    for p in range(out.shape[0]):
        out[p] = s1


def post2_body(red1, red2, u0, s1, t2, out):
    beta, _, comb = scalars([red_rows(red1, 3), red_rows(red2, 3)])
    (c0, c1), h = comb[1]
    s2 = (t2[...] - c0 * (u0[0] / beta) - c1 * s1[0]) / h
    for p in range(out.shape[0]):
        out[p] = s2


def post3_body(red1, red2, red3, mine, u0, s1, s2, t3, basis, out):
    beta, _, comb = scalars([red_rows(red1, 3), red_rows(red2, 3), red_rows(red3, 4)])
    (b0,), h1 = comb[0]
    (c0, c1), h2 = comb[1]
    (d0, d1, d2), h3 = comb[2]
    v0 = mine[4:8] / beta
    s0 = u0[0] / beta
    v1 = (s0 - b0 * v0) / h1
    v2 = (s1[0] - c0 * v0 - c1 * v1) / h2
    v3 = (s2[0] - d0 * v0 - d1 * v1 - d2 * v2) / h3
    s3 = (t3[...] - d0 * s0 - d1 * s1[0] - d2 * s2[0]) / h3
    for k, v in enumerate([v0, v1, v2, v3]):
        basis[k] = v
    put_sums(out, [total(s3 * v) for v in (v0, v1, v2, v3)] + [total(s3 * s3)])


def cells_body(centre, red1, red2, red3, own, group, right, v1, v2, s2, out, left, acc):
    beta, _, comb = scalars([red_rows(red1, 3), red_rows(red2, 3), red_rows(red3, 4)])
    (d0, d1, d2), h3 = comb[2]
    cells = own.shape[0]
    used = out.shape[3]
    width = own.shape[2]
    row = row_of(width)
    shift = jnp.where(row == 0, centre[0], 0.0)
    for i in range(cells):
        left[i * used : (i + 1) * used, :] = target_rows(own[i] - shift)[:used]
    acc[...] = jnp.zeros_like(acc)

    def step(s, _):
        pts = group[s]
        area = SCALE * pts[3:4]
        v0 = pts[4:8] / beta
        a1, a2 = v1[s], v2[s]
        a3 = (s2[s] - d0 * v0 - d1 * a1 - d2 * a2) / h3
        rows = []
        for pair in ((v0, a1), (a2, a3)):
            thirds = []
            for v in pair:
                four = area * v
                p, q, t = moment_rows(pts, jnp.concatenate([four, four], axis=0))
                rows += [p, q]
                thirds.append(t)
            rows.append(thirds[0] + pltpu.roll(thirds[1], 4, 0))
        accumulate(acc, left, right[s], moment_block(rows), blocks_of(cells * used, used // 2), HILO_CELLS)
        return 0

    lax.fori_loop(0, group.shape[0], step, 0)
    for i in range(cells):
        pts = own[i] - shift
        full = jnp.concatenate([acc[i * used : (i + 1) * used, :], jnp.zeros((width - used, 256), F32)], axis=0)
        rows = jnp.transpose(full)
        rows = rows[0:80] + rows[80:160] + rows[160:240]
        for k in range(4):
            at, half = 40 * (k // 2), k % 2
            p, q = rows[at + 16 * half : at + 16 * half + 8], rows[at + 16 * half + 8 : at + 16 * half + 16]
            e = rows[at + 32 + 4 * half : at + 36 + 4 * half]
            vel = assemble(pts, p[0:4], p[4:8], q[0:4], q[4:8], e)
            out[k, i] = vel[0:3, :used]


def last_body(red1, red2, red3, red4, basis, near, wall, velocity_out, density_out):
    reds = [red_rows(red1, 3), red_rows(red2, 3), red_rows(red3, 4), red_rows(red4, 5)]
    beta, hess, _ = scalars(reds)
    y = solve_small(hess, beta, 4)
    density = y[0] * basis[0]
    for k in range(1, 4):
        density = density + y[k] * basis[k]
    density_out[...] = density[0:3]
    for i in range(near.shape[0]):
        part = y[0] * wall[0, i]
        for k in range(1, 4):
            part = part + y[k] * wall[k, i]
        velocity_out[i] = near[i] + part


HILO = True
HILO_CELLS = True


def swap(x, axes):
    return lax.all_to_all(x, axes, 0, 0, tiled=True)


def per_device(cell_points, cell_force, cell_weight, partners, wall_points, wall_area, wall_data):
    cells, _, surface = cell_points.shape
    points = wall_points.shape[1]
    segments, peers = lax.axis_size("wall"), lax.axis_size("cell")
    width = -(-surface // 128) * 128
    centre = 8.0 * lax.axis_index("wall").astype(F32) + 4.0

    strength = cell_force * cell_weight[:, None, :]
    gap = jnp.zeros((cells, 1, surface), F32)
    own = jnp.concatenate([cell_points, gap, strength, gap], axis=1)
    own = jnp.pad(own, ((0, 0), (0, 0), (0, width - surface)))
    shift = jnp.stack([centre, jnp.zeros_like(centre), jnp.zeros_like(centre)])
    mine = jnp.concatenate(
        [wall_points - shift[:, None], wall_area[None], wall_data, jnp.zeros((1, points), F32)], axis=0
    )
    group = swap(jnp.broadcast_to(mine[None], (peers, *mine.shape)), "cell")
    everyone = swap(jnp.broadcast_to(own[None], (peers, *own.shape)), "cell")

    wall_scratch = (pltpu.VMEM((points, 48), BF16), pltpu.VMEM((points, 128), F32))
    copies = shape(peers, 4, points)
    sums = shape(segments, 8, 128)

    right, u0 = call(
        first_body, [shape(peers, 48, points, dtype=BF16), copies], (mine, group), "first", wall_scratch
    )
    u0_all = swap(u0, "cell")
    near = call(
        near_body,
        shape(cells, 3, surface),
        (partners, own, everyone),
        "near",
        (
            pltpu.VMEM((width, 48), BF16),
            pltpu.VMEM((width, 128), F32),
            pltpu.VMEM((8, (partners.shape[1] + 2) * width), F32),
        ),
        smem=(0,),
    )

    def apply(vector):
        return call(apply_body, shape(4, points), (mine, group, right, vector), "apply", wall_scratch)

    red1 = swap(call(pre1_body, sums, (group, u0_all), "pre1"), "wall")
    t1 = apply(u0_all)
    s1 = call(post1_body, copies, (red1, u0, t1), "post1")
    s1_all = swap(s1, "cell")
    v1, sum2 = call(pre2_body, [copies, sums], (red1, group, u0_all, s1_all), "pre2")
    red2 = swap(sum2, "wall")
    t2 = apply(s1_all)
    s2 = call(post2_body, copies, (red1, red2, u0, s1, t2), "post2")
    s2_all = swap(s2, "cell")
    v2, sum3 = call(pre3_body, [copies, sums], (red1, red2, group, v1, s1_all, s2_all), "pre3")
    red3 = swap(sum3, "wall")
    t3 = apply(s2_all)
    basis, sum4 = call(
        post3_body,
        [shape(4, 4, points), shape(segments * peers, 8, 128)],
        (red1, red2, red3, mine, u0, s1, s2, t3),
        "post3",
    )
    red4 = swap(sum4, AXES)
    wall = call(
        cells_body,
        shape(4, cells, 3, surface),
        (centre[None], red1, red2, red3, own, group, right, v1, v2, s2_all),
        "cells",
        (pltpu.VMEM((cells * surface, 48), BF16), pltpu.VMEM((cells * surface, 256), F32)),
        smem=(0,),
    )
    velocity_out, density = call(
        last_body,
        [shape(cells, 3, surface), shape(3, points)],
        (red1, red2, red3, red4, basis, near, wall),
        "last",
    )
    return velocity_out, density


def solution(mesh):
    in_specs = (
        P(AXES, None, None),
        P(AXES, None, None),
        P(AXES, None),
        P(AXES, None),
        P(None, AXES),
        P(AXES),
        P(None, AXES),
    )
    out_specs = (P(AXES, None, None), P(None, AXES))
    return jax.shard_map(per_device, mesh=mesh, in_specs=in_specs, out_specs=out_specs, check_vma=False)
```

```python
import math

import jax
import jax.numpy as jnp
from jax import lax
from jax.experimental import pallas as pl
from jax.experimental.pallas import tpu as pltpu
from jax.sharding import PartitionSpec as P

F32 = jnp.float32
BF16 = jnp.bfloat16
AXES = ("wall", "cell")
E2 = 0.1 * 0.1
FLOOR = 1e-06
SCALE = 1.0 / (8.0 * math.pi)
VMEM_LIMIT = 40 * 2**20


def row_of(n):
    return lax.broadcasted_iota(jnp.int32, (8, n), 0)


def split3(a):
    high = a.astype(BF16).astype(F32)
    rest = a - high
    mid = rest.astype(BF16).astype(F32)
    low = (rest - mid).astype(BF16).astype(F32)
    return high, mid, low


def target_factor(points):
    row = row_of(points.shape[1])
    coords = jnp.where(row < 3, points, 0.0)
    norm2 = jnp.sum(coords * coords, axis=0, keepdims=True) + E2
    eight = jnp.where(row < 3, -2.0 * coords, jnp.where(row == 3, 1.0, jnp.where(row == 4, norm2, 0.0)))
    h, m, l = split3(eight)
    return jnp.concatenate([h, m, l, h, m, h], axis=0)


def source_factor(points):
    row = row_of(points.shape[1])
    coords = jnp.where(row < 3, points, 0.0)
    norm2 = jnp.sum(coords * coords, axis=0, keepdims=True)
    eight = jnp.where(row < 3, coords, jnp.where(row == 3, norm2, jnp.where(row == 4, 1.0, 0.0)))
    h, m, l = split3(eight)
    return jnp.concatenate([h, h, h, m, m, l], axis=0)


def upright(a):
    wide = jnp.concatenate([a, jnp.zeros((128 - a.shape[0], a.shape[1]), F32)], axis=0)
    return jnp.transpose(wide)[:, : a.shape[0]].astype(BF16)


def moment_rows(points, twice):
    row = row_of(points.shape[1])
    coords = jnp.where(row < 3, points, 0.0)
    y0, y1, y2 = points[0:1], points[1:2], points[2:3]
    norm2 = jnp.sum(coords * coords, axis=0, keepdims=True)
    inner = jnp.sum(coords * twice, axis=0, keepdims=True)
    e = norm2 * twice + inner * coords
    first = twice * jnp.where(row < 4, 1.0, y0)
    first = jnp.where(row == 3, e[0:1], jnp.where(row == 7, e[1:2], first))
    second = twice * jnp.where(row < 4, y1, y2)
    second = jnp.where(row == 3, e[2:3], second)
    return [first, second]


def moment_block(groups):
    parts = [split3(g) for g in groups]
    return jnp.concatenate([p[k] for k in range(3) for p in parts], axis=0).astype(BF16)


def kernel_values(shifted, hilo):
    inv = lax.rsqrt(shifted)
    kern = inv * inv * inv
    high = kern.astype(BF16)
    return [high, (kern - high.astype(F32)).astype(BF16)] if hilo else [high]


def add_chunk(acc, sources, targets, moments, hilo):
    parts = kernel_values(jnp.dot(sources, targets, preferred_element_type=F32), hilo)
    acc[...] += jnp.dot(moments, parts[0], preferred_element_type=F32)
    if hilo:
        acc[0:32, :] += jnp.dot(moments[0:32], parts[1], preferred_element_type=F32)
    return parts[0]


def assemble(points, rows):
    f, t0, t1, t2 = rows[0:4], rows[4:8], rows[8:12], rows[12:16]
    n = points.shape[1]
    row = lax.broadcasted_iota(jnp.int32, (4, n), 0)
    x4 = jnp.where(row < 3, points[0:4], 0.0)
    x0, x1, x2 = x4[0:1], x4[1:2], x4[2:3]
    norm2 = jnp.sum(x4 * x4, axis=0, keepdims=True)
    along = jnp.sum(x4 * f, axis=0, keepdims=True) - (t0[0:1] + t1[1:2] + t2[2:3])
    s0 = jnp.sum(x4 * t0, axis=0, keepdims=True)
    s1 = jnp.sum(x4 * t1, axis=0, keepdims=True)
    s2 = jnp.sum(x4 * t2, axis=0, keepdims=True)
    e = jnp.where(row == 0, f[3:4] - s0, jnp.where(row == 1, t0[3:4] - s1, t1[3:4] - s2))
    return jnp.where(row < 3, (norm2 + 2.0 * E2) * f + e - 2.0 * (x0 * t0 + x1 * t1 + x2 * t2) + x4 * along, 0.0)


def velocity(points, acc):
    return assemble(points, acc[0:16] + acc[16:32] + acc[32:48])


def solve_small(hess, beta, size):
    zero = jnp.zeros_like(beta)
    upper = [[hess.get((r, c), zero) for c in range(size)] for r in range(size + 1)]
    targets = [beta] + [zero] * size
    cosines, sines = [], []
    for column in range(size):
        for prior in range(column):
            a, b = upper[prior][column], upper[prior + 1][column]
            upper[prior][column] = cosines[prior] * a + sines[prior] * b
            upper[prior + 1][column] = cosines[prior] * b - sines[prior] * a
        a, b = upper[column][column], upper[column + 1][column]
        radius = jnp.sqrt(a * a + b * b)
        cosines.append(a / radius)
        sines.append(b / radius)
        upper[column][column] = radius
        targets[column + 1] = -sines[column] * targets[column]
        targets[column] = cosines[column] * targets[column]
    weights = [None] * size
    for column in reversed(range(size)):
        part = targets[column]
        for later in range(column + 1, size):
            part = part - upper[column][later] * weights[later]
        weights[column] = part / upper[column][column]
    return weights


def row_with(values, start):
    lane = lax.broadcasted_iota(jnp.int32, (1, 128), 1)
    row = jnp.zeros((1, 128), F32)
    for k, v in enumerate(values):
        row = jnp.where(lane == start + k, jnp.broadcast_to(v, (1, 128)), row)
    return row


def total(a):
    while a.ndim > 2:
        a = jnp.sum(a, axis=0)
    return jnp.sum(jnp.sum(a, axis=0, keepdims=True), axis=1, keepdims=True)


def call(body, outs, ins, name, scratch=(), smem=(), apart=(), apart_out=()):
    def whole(dims):
        return pl.BlockSpec(dims, lambda i: (0,) * len(dims))

    in_specs = []
    for k, x in enumerate(ins):
        if k in smem:
            in_specs.append(pl.BlockSpec(memory_space=pltpu.SMEM))
        elif k in apart:
            in_specs.append(pl.BlockSpec(memory_space=pltpu.HBM))
        else:
            in_specs.append(whole(x.shape))
    out_specs = [
        pl.BlockSpec(memory_space=pltpu.HBM) if k in apart_out else whole(x.shape) for k, x in enumerate(outs)
    ]
    return pl.pallas_call(
        body,
        grid=(1,),
        out_shape=outs,
        in_specs=in_specs,
        out_specs=out_specs,
        scratch_shapes=list(scratch),
        compiler_params=pltpu.CompilerParams(vmem_limit_bytes=VMEM_LIMIT),
        name=name,
    )(*ins)


def shape(*dims, dtype=F32):
    return jax.ShapeDtypeStruct(dims, dtype)


def pack_body(centre, *refs):
    count = 6
    given, (mine, own, sent_wall, sent_cells) = refs[:count], refs[count : count + 4]
    held, sems = refs[count + 4 : 2 * count + 4], refs[2 * count + 4]
    moves = [pltpu.make_async_copy(x, y, sems.at[k]) for k, (x, y) in enumerate(zip(given, held))]
    for m in moves:
        m.start()
    for m in moves:
        m.wait()
    points, area, data, cell_points, cell_force, cell_weight = held
    n = points.shape[1]
    row = lax.broadcasted_iota(jnp.int32, (3, n), 0)
    mine[0:3] = points[...] - jnp.where(row == 0, centre[0], 0.0)
    mine[3:4] = area[...]
    mine[4:7] = data[...]
    mine[7:8] = jnp.zeros((1, n), F32)
    used = cell_points.shape[2]
    own[...] = jnp.zeros_like(own)
    for i in range(own.shape[0]):
        own[i, 0:3, 0:used] = cell_points[:, i, :]
        own[i, 4:7, 0:used] = cell_force[:, i, :] * cell_weight[i : i + 1, :]
    for p in range(sent_wall.shape[0]):
        sent_wall[p] = mine[...]
        sent_cells[p] = own[...]


def near_body(first, partners, own, everyone, out, sources, acc):
    cells = own.shape[0]
    width = own.shape[2]
    used = out.shape[2]
    row = row_of(width)
    r = row_of(THREE * width)
    for i in range(cells):
        mine = own[i]
        centre = jnp.where(row < 3, mine[:, 0:1], 0.0)
        for k in range(THREE):
            slot = first + k
            if slot == 0:
                sources[:, 0:width] = mine - centre
                continue
            n = partners[i, slot - 1]
            there = jnp.maximum(n, 0)
            other = everyone[there // cells, there % cells] - centre
            keep = jnp.where(n >= 0, 1.0, 0.0)
            sources[:, k * width : (k + 1) * width] = jnp.where(row >= 4, other * keep, other)
        targets = target_factor(mine - centre).astype(BF16)[:, :used]
        pts = sources[...]
        twice = SCALE * jnp.where(r >= 4, pts, pltpu.roll(pts, 4, 0))
        acc[...] = jnp.zeros_like(acc)
        add_chunk(acc, upright(source_factor(pts)), targets, moment_block(moment_rows(pts, twice)), True)
        out[i] = velocity((mine - centre)[:, :used], acc[...])


def parcels(near, far, sems, inward):
    n = near.shape[0] // PARCELS
    moves = []
    for k in range(PARCELS):
        here, there = near.at[pl.ds(k * n, n)], far.at[pl.ds(k * n, n)]
        moves.append(pltpu.make_async_copy(*((there, here) if inward else (here, there)), sems.at[k]))
    return n, moves


def first_body(mine, group, store, out, state, kept, acc, sems):
    targets = target_factor(mine[...]).astype(BF16)
    row = row_of(mine.shape[1])
    norm2 = total(jnp.where(row >= 4, group[...] * group[...], 0.0))
    size = jnp.sqrt(norm2 + TINY)
    state[...] = row_with([size, norm2 / (size * size)], 0)
    acc[...] = jnp.zeros_like(acc)

    def step(c, _):
        pts = group[c]
        twice = (SCALE * pts[3:4] / size) * jnp.where(row >= 4, pts, pltpu.roll(pts, 4, 0))
        moments = moment_block(moment_rows(pts, twice))
        kept[c] = add_chunk(acc, upright(source_factor(pts)), targets, moments, HILO_FIRST)
        return 0

    n, moves = parcels(kept, store, sems, False)
    for k, move in enumerate(moves):
        lax.fori_loop(k * n, (k + 1) * n, step, 0)
        move.start()
    vel = velocity(mine[...], acc[...])
    for p in range(out.shape[0]):
        out[p] = vel
    for move in moves:
        move.wait()


def fetch(store, kept, sems):
    n, moves = parcels(kept, store, sems, True)
    for move in moves:
        move.start()


def next_vector(group, state0, earlier, image, vector):
    basis = [data_rows(group[...]) / state0[0:1, 0:1]] + [q[...] for q in earlier]
    s = image[...]
    inner = [total(s * q) for q in basis]
    for b, q in zip(inner, basis):
        s = s - b * q
    norm2 = total(s * s)
    size = jnp.sqrt(norm2 + TINY)
    vector[...] = s / size
    return inner + [size, norm2 / (size * size)]


def apply_vector(mine, group, store, vector, kept, acc, sems):
    acc[...] = jnp.zeros_like(acc)

    def step(c, _):
        pts = group[c]
        four = vector[c] * (SCALE * pts[3:4])
        moments = moment_block(moment_rows(pts, jnp.concatenate([four, four], axis=0)))
        acc[...] += jnp.dot(moments, kept[c], preferred_element_type=F32)
        return 0

    n, moves = parcels(kept, store, sems, True)
    for k, move in enumerate(moves):
        move.wait()
        lax.fori_loop(k * n, (k + 1) * n, step, 0)
    return velocity(mine[...], acc[...])


def second_body(mine, group, store, state0, image, after, vector, out, state, kept, acc, sems):
    fetch(store, kept, sems)
    state[...] = row_with(next_vector(group, state0, [], image, vector), 2)
    vel = apply_vector(mine, group, store, vector, kept, acc, sems)
    for p in range(out.shape[0]):
        out[p] = vel


def third_body(mine, group, store, state0, q1, image, after, vector, out, state, kept, acc, sems):
    fetch(store, kept, sems)
    state[...] = row_with(next_vector(group, state0, [q1], image, vector), 5)
    vel = apply_vector(mine, group, store, vector, kept, acc, sems)
    for p in range(out.shape[0]):
        out[p] = vel


def fourth_body(at, mine, group, store, state0, state1, state2, q1, q2, image, after, vector, basis, out, kept, acc, sems):
    fetch(store, kept, sems)
    state3 = row_with(next_vector(group, state0, [q1, q2], image, vector), 9)
    vel = apply_vector(mine, group, store, vector, kept, acc, sems)
    own = [mine[4:8] / state0[0:1, 0:1]] + [q[at[0]] for q in (q1, q2, vector)]
    for k, q in enumerate(own):
        basis[k] = q
    last = row_with([total(vel * q) for q in own] + [total(vel * vel)], 14)
    out[...] = jnp.broadcast_to(state0[...] + state1[...] + state2[...] + state3 + last, out.shape)


def data_rows(block):
    return block[:, 4:8, :]


def cells_body(centre, state0, own, group, q1, q2, q3, out, left, acc):
    used = out.shape[3]
    width = own.shape[2]
    shift = jnp.where(row_of(width) == 0, centre[0], 0.0)
    size = state0[0:1, 0:1]
    cells = own.shape[0]
    for i in range(cells):
        left[i * used : (i + 1) * used, :] = upright(target_factor(own[i] - shift))[:used]
    acc[...] = jnp.zeros_like(acc)

    def step(c, _):
        pts = group[c]
        area = SCALE * pts[3:4]
        groups = []
        for v in (pts[4:8] / size, q1[c], q2[c], q3[c]):
            four = area * v
            groups += moment_rows(pts, jnp.concatenate([four, four], axis=0))
        moments = moment_block(groups)
        shifted = jnp.dot(left[...], source_factor(pts).astype(BF16), preferred_element_type=F32)
        for part in kernel_values(shifted, HILO_CELLS):
            acc[...] += lax.dot_general(part, moments, (((1,), (1,)), ((), ())), preferred_element_type=F32)
        return 0

    lax.fori_loop(0, group.shape[0], step, 0)
    for i in range(cells):
        part = acc[i * used : (i + 1) * used, :]
        full = jnp.concatenate([part, jnp.zeros((width - used, part.shape[1]), F32)], axis=0)
        full = jnp.concatenate([full, jnp.zeros((width, 256 - part.shape[1]), F32)], axis=1)
        rows = jnp.transpose(full)
        for k in range(4):
            sums = rows[16 * k : 16 * k + 16] + rows[64 + 16 * k : 80 + 16 * k] + rows[128 + 16 * k : 144 + 16 * k]
            out[k, i] = assemble(own[i] - shift, sums)[:, :used]


def krylov(local, gram, start, size):
    def dot(a, b):
        return sum(jnp.sum(gram[k] * x * y, axis=0, keepdims=True) for k, (x, y) in enumerate(zip(a, b)))

    beta = jnp.sqrt(dot([start], [start]) + FLOOR)
    basis = [[start / beta]]
    hess = {}
    for j in range(size):
        v = basis[j]
        w = []
        for k in range(j + 2):
            part = sum(local[(k, m)] * v[m] for m in range(max(k - 1, 0), j + 1))
            w.append(0.5 * v[k] + part if k <= j else part)
        for i in range(j + 1):
            h = dot(w, basis[i])
            hess[(i, j)] = h
            w = [x - h * basis[i][k] if k <= i else x for k, x in enumerate(w)]
        h = jnp.sqrt(dot(w, w) + FLOOR)
        hess[(j + 1, j)] = h
        basis.append([x / h for x in w])
    y = solve_small(hess, beta, size)
    return [sum(y[j] * basis[j][k] for j in range(k, size)) for k in range(size)]


def last_body(at, red, basis, near0, near1, near2, wall, velocity_out, density_out):
    segments = 8
    peers = red.shape[0] // segments
    rows = [jnp.sum(red[s * peers : (s + 1) * peers, :], axis=0, keepdims=True) for s in range(segments)]
    table = jnp.concatenate(rows, axis=0)
    same = lambda k: table[:, k : k + 1] * (1.0 / peers)
    local, gram = {}, [same(1)]
    start = same(0)
    for m, first in ((0, 2), (1, 5), (2, 9)):
        for k in range(m + 2):
            local[(k, m)] = same(first + k)
        gram.append(same(first + m + 2))
    norm2 = table[:, 18:19]
    for k in range(4):
        inner = table[:, 14 + k : 15 + k]
        local[(k, 3)] = inner
        norm2 = norm2 - inner * inner * (2.0 - gram[k])
    norm2 = jnp.maximum(norm2, 0.0)
    size = jnp.sqrt(norm2 + TINY)
    local[(4, 3)] = size
    gram.append(norm2 / (size * size))
    coords = krylov(local, gram, start, 4)
    mine = lax.broadcasted_iota(jnp.int32, (segments, 1), 0) == at[0]
    z = [jnp.sum(jnp.where(mine, x, 0.0), axis=0, keepdims=True) for x in coords]
    density = z[0] * basis[0]
    for k in range(1, 4):
        density = density + z[k] * basis[k]
    density_out[...] = density[0:3]
    for i in range(near0.shape[0]):
        part = near0[i] + near1[i] + near2[i]
        for k in range(4):
            part = part + z[k] * wall[k, i]
        velocity_out[:, i, :] = part[0:3]


HILO_FIRST = True
HILO = False
HILO_CELLS = False
TINY = 1e-30
THREE = 3
PARCELS = 4


def swap(x, axes):
    return lax.all_to_all(x, axes, 0, 0, tiled=True)


def per_device(cell_points, cell_force, cell_weight, partners, wall_points, wall_area, wall_data):
    cells, _, surface = cell_points.shape
    points = wall_points.shape[1]
    segments, peers = lax.axis_size("wall"), lax.axis_size("cell")
    width = -(-surface // 128) * 128
    segment = lax.axis_index("wall")
    centre = 8.0 * segment.astype(F32) + 4.0
    at = lax.axis_index("cell").astype(jnp.int32)[None]

    copies = shape(peers, 4, points)
    row = shape(1, 128)
    given = (
        wall_points,
        wall_area[None],
        wall_data,
        jnp.transpose(cell_points, (1, 0, 2)),
        jnp.transpose(cell_force, (1, 0, 2)),
        cell_weight,
    )
    mine, own, sent_wall, sent_cells = call(
        pack_body,
        [shape(8, points), shape(cells, 8, width), shape(peers, 8, points), shape(peers, cells, 8, width)],
        (centre[None], *given),
        "pack",
        [pltpu.VMEM(x.shape, F32) for x in given] + [pltpu.SemaphoreType.DMA((len(given),))],
        smem=(0,),
        apart=range(1, 1 + len(given)),
    )
    group = swap(sent_wall, "cell")
    everyone = swap(sent_cells, "cell")
    scratch = (
        pltpu.VMEM((peers, points, points), BF16),
        pltpu.VMEM((48, points), F32),
        pltpu.SemaphoreType.DMA((PARCELS,)),
    )

    def near(k):
        return call(
            lambda *refs: near_body(THREE * k, *refs),
            [shape(cells, 4, surface)],
            (partners, own, everyone),
            "near" + str(k),
            (pltpu.VMEM((8, THREE * width), F32), pltpu.VMEM((48, surface), F32)),
            smem=(0,),
        )[0]

    store, s0, state0 = call(
        first_body,
        [shape(peers, points, points, dtype=BF16), copies, row],
        (mine, group),
        "first",
        scratch,
        apart_out=(0,),
    )
    near0 = near(0)
    q1, s1, state1 = call(
        second_body,
        [copies, copies, row],
        (mine, group, store, state0, swap(s0, "cell"), near0),
        "second",
        scratch,
        apart=(2, 5),
    )
    near1 = near(1)
    q2, s2, state2 = call(
        third_body,
        [copies, copies, row],
        (mine, group, store, state0, q1, swap(s1, "cell"), near1),
        "third",
        scratch,
        apart=(2, 6),
    )
    near2 = near(2)
    q3, basis, sums = call(
        fourth_body,
        [copies, shape(4, 4, points), shape(segments * peers, 128)],
        (at, mine, group, store, state0, state1, state2, q1, q2, swap(s2, "cell"), near2),
        "fourth",
        scratch,
        smem=(0,),
        apart=(3, 10),
    )
    red = swap(sums, AXES)
    (wall,) = call(
        cells_body,
        [shape(4, cells, 4, surface)],
        (centre[None], state0, own, group, q1, q2, q3),
        "cells",
        (pltpu.VMEM((cells * surface, 48), BF16), pltpu.VMEM((cells * surface, 192), F32)),
        smem=(0,),
    )
    velocity_out, density = call(
        last_body,
        [shape(3, cells, surface), shape(3, points)],
        (segment.astype(jnp.int32)[None], red, basis, near0, near1, near2, wall),
        "last",
        smem=(0,),
    )
    return jnp.transpose(velocity_out, (1, 0, 2)), density


def solution(mesh):
    in_specs = (
        P(AXES, None, None),
        P(AXES, None, None),
        P(AXES, None),
        P(AXES, None),
        P(None, AXES),
        P(AXES),
        P(None, AXES),
    )
    out_specs = (P(AXES, None, None), P(None, AXES))
    step = jax.shard_map(per_device, mesh=mesh, in_specs=in_specs, out_specs=out_specs, check_vma=False)
    return step
```

```python
import math

import jax
import jax.numpy as jnp
from jax import lax
from jax.experimental import pallas as pl
from jax.experimental.pallas import tpu as pltpu
from jax.sharding import PartitionSpec as P

F32 = jnp.float32
BF16 = jnp.bfloat16
AXES = ("wall", "cell")
E2 = 0.1 * 0.1
FLOOR = 1e-06
SCALE = 1.0 / (8.0 * math.pi)
VMEM_LIMIT = 48 * 2**20


def row_of(n):
    return lax.broadcasted_iota(jnp.int32, (8, n), 0)


def split3(a):
    high = a.astype(BF16).astype(F32)
    rest = a - high
    mid = rest.astype(BF16).astype(F32)
    low = (rest - mid).astype(BF16).astype(F32)
    return high, mid, low


def target_factor(points):
    row = row_of(points.shape[1])
    coords = jnp.where(row < 3, points, 0.0)
    norm2 = jnp.sum(coords * coords, axis=0, keepdims=True) + E2
    eight = jnp.where(row < 3, -2.0 * coords, jnp.where(row == 3, 1.0, jnp.where(row == 4, norm2, 0.0)))
    h, m, l = split3(eight)
    return jnp.concatenate([h, m, l, h, m, h], axis=0)


def source_factor(points):
    row = row_of(points.shape[1])
    coords = jnp.where(row < 3, points, 0.0)
    norm2 = jnp.sum(coords * coords, axis=0, keepdims=True)
    eight = jnp.where(row < 3, coords, jnp.where(row == 3, norm2, jnp.where(row == 4, 1.0, 0.0)))
    h, m, l = split3(eight)
    return jnp.concatenate([h, h, h, m, m, l], axis=0)


def upright(a):
    wide = jnp.concatenate([a, jnp.zeros((128 - a.shape[0], a.shape[1]), F32)], axis=0)
    return jnp.transpose(wide)[:, : a.shape[0]].astype(BF16)


def moment_rows(points, twice):
    row = row_of(points.shape[1])
    coords = jnp.where(row < 3, points, 0.0)
    y0, y1, y2 = points[0:1], points[1:2], points[2:3]
    norm2 = jnp.sum(coords * coords, axis=0, keepdims=True)
    inner = jnp.sum(coords * twice, axis=0, keepdims=True)
    e = norm2 * twice + inner * coords
    first = twice * jnp.where(row < 4, 1.0, y0)
    first = jnp.where(row == 3, e[0:1], jnp.where(row == 7, e[1:2], first))
    second = twice * jnp.where(row < 4, y1, y2)
    second = jnp.where(row == 3, e[2:3], second)
    return [first, second]


def moment_block(groups):
    parts = [split3(g) for g in groups]
    return jnp.concatenate([p[k] for k in range(3) for p in parts], axis=0).astype(BF16)


def kernel_values(shifted, hilo):
    inv = lax.rsqrt(shifted)
    kern = inv * inv * inv
    high = kern.astype(BF16)
    return [high, (kern - high.astype(F32)).astype(BF16)] if hilo else [high]


def add_chunk(acc, sources, targets, moments, hilo):
    parts = kernel_values(jnp.dot(sources, targets, preferred_element_type=F32), hilo)
    acc[...] += jnp.dot(moments, parts[0], preferred_element_type=F32)
    if hilo:
        acc[0:32, :] += jnp.dot(moments[0:32], parts[1], preferred_element_type=F32)
    return parts[0]


def assemble(points, rows):
    f, t0, t1, t2 = rows[0:4], rows[4:8], rows[8:12], rows[12:16]
    n = points.shape[1]
    row = lax.broadcasted_iota(jnp.int32, (4, n), 0)
    x4 = jnp.where(row < 3, points[0:4], 0.0)
    x0, x1, x2 = x4[0:1], x4[1:2], x4[2:3]
    norm2 = jnp.sum(x4 * x4, axis=0, keepdims=True)
    along = jnp.sum(x4 * f, axis=0, keepdims=True) - (t0[0:1] + t1[1:2] + t2[2:3])
    s0 = jnp.sum(x4 * t0, axis=0, keepdims=True)
    s1 = jnp.sum(x4 * t1, axis=0, keepdims=True)
    s2 = jnp.sum(x4 * t2, axis=0, keepdims=True)
    e = jnp.where(row == 0, f[3:4] - s0, jnp.where(row == 1, t0[3:4] - s1, t1[3:4] - s2))
    return jnp.where(row < 3, (norm2 + 2.0 * E2) * f + e - 2.0 * (x0 * t0 + x1 * t1 + x2 * t2) + x4 * along, 0.0)


def velocity(points, acc):
    return assemble(points, acc[0:16] + acc[16:32] + acc[32:48])


def solve_small(hess, beta, size):
    zero = jnp.zeros_like(beta)
    upper = [[hess.get((r, c), zero) for c in range(size)] for r in range(size + 1)]
    targets = [beta] + [zero] * size
    cosines, sines = [], []
    for column in range(size):
        for prior in range(column):
            a, b = upper[prior][column], upper[prior + 1][column]
            upper[prior][column] = cosines[prior] * a + sines[prior] * b
            upper[prior + 1][column] = cosines[prior] * b - sines[prior] * a
        a, b = upper[column][column], upper[column + 1][column]
        radius = jnp.sqrt(a * a + b * b)
        cosines.append(a / radius)
        sines.append(b / radius)
        upper[column][column] = radius
        targets[column + 1] = -sines[column] * targets[column]
        targets[column] = cosines[column] * targets[column]
    weights = [None] * size
    for column in reversed(range(size)):
        part = targets[column]
        for later in range(column + 1, size):
            part = part - upper[column][later] * weights[later]
        weights[column] = part / upper[column][column]
    return weights


def row_with(values, start):
    lane = lax.broadcasted_iota(jnp.int32, (1, 128), 1)
    row = jnp.zeros((1, 128), F32)
    for k, v in enumerate(values):
        row = jnp.where(lane == start + k, jnp.broadcast_to(v, (1, 128)), row)
    return row


def total(a):
    while a.ndim > 2:
        a = jnp.sum(a, axis=0)
    return jnp.sum(jnp.sum(a, axis=0, keepdims=True), axis=1, keepdims=True)


def call(body, outs, ins, name, scratch=(), smem=(), apart=(), apart_out=()):
    def whole(dims):
        return pl.BlockSpec(dims, lambda i: (0,) * len(dims))

    in_specs = []
    for k, x in enumerate(ins):
        if k in smem:
            in_specs.append(pl.BlockSpec(memory_space=pltpu.SMEM))
        elif k in apart:
            in_specs.append(pl.BlockSpec(memory_space=pltpu.HBM))
        else:
            in_specs.append(whole(x.shape))
    out_specs = [
        pl.BlockSpec(memory_space=pltpu.HBM) if k in apart_out else whole(x.shape) for k, x in enumerate(outs)
    ]
    return pl.pallas_call(
        body,
        grid=(1,),
        out_shape=outs,
        in_specs=in_specs,
        out_specs=out_specs,
        scratch_shapes=list(scratch),
        compiler_params=pltpu.CompilerParams(vmem_limit_bytes=VMEM_LIMIT),
        name=name,
    )(*ins)


def shape(*dims, dtype=F32):
    return jax.ShapeDtypeStruct(dims, dtype)


def pack_body(centre, *refs):
    count = 6
    given, (mine, own, sent_wall, sent_cells) = refs[:count], refs[count : count + 4]
    held, sems = refs[count + 4 : 2 * count + 4], refs[2 * count + 4]
    moves = [pltpu.make_async_copy(x, y, sems.at[k]) for k, (x, y) in enumerate(zip(given, held))]
    for m in moves:
        m.start()
    for m in moves:
        m.wait()
    points, area, data, cell_points, cell_force, cell_weight = held
    n = points.shape[1]
    row = lax.broadcasted_iota(jnp.int32, (3, n), 0)
    mine[0:3] = points[...] - jnp.where(row == 0, centre[0], 0.0)
    mine[3:4] = jnp.concatenate([area[k : k + 1] for k in range(area.shape[0])], axis=1)
    mine[4:7] = data[...]
    mine[7:8] = jnp.zeros((1, n), F32)
    used = cell_points.shape[2]
    own[...] = jnp.zeros_like(own)
    for i in range(own.shape[0]):
        own[i, 0:3, 0:used] = cell_points[:, i, :]
        own[i, 4:7, 0:used] = cell_force[:, i, :] * cell_weight[i : i + 1, :]
    for p in range(sent_wall.shape[0]):
        sent_wall[p] = mine[...]
        sent_cells[p] = own[...]


def near_body(first, partners, own, everyone, out, sources, acc):
    cells = own.shape[0]
    width = own.shape[2]
    used = out.shape[2]
    row = row_of(width)
    r = row_of(THREE * width)
    for i in range(cells):
        mine = own[i]
        centre = jnp.where(row < 3, mine[:, 0:1], 0.0)
        for k in range(THREE):
            slot = first + k
            if slot == 0:
                sources[:, 0:width] = mine - centre
                continue
            n = partners[i, slot - 1]
            there = jnp.maximum(n, 0)
            other = everyone[there // cells, there % cells] - centre
            keep = jnp.where(n >= 0, 1.0, 0.0)
            sources[:, k * width : (k + 1) * width] = jnp.where(row >= 4, other * keep, other)
        targets = target_factor(mine - centre).astype(BF16)[:, :used]
        pts = sources[...]
        twice = SCALE * jnp.where(r >= 4, pts, pltpu.roll(pts, 4, 0))
        acc[...] = jnp.zeros_like(acc)
        add_chunk(acc, upright(source_factor(pts)), targets, moment_block(moment_rows(pts, twice)), True)
        out[i] = velocity((mine - centre)[:, :used], acc[...])


def parcel(near, far, sems, k, inward):
    here, there = near.at[pl.ds(k * PART, PART)], far.at[pl.ds(k * PART, PART)]
    return pltpu.make_async_copy(*((there, here) if inward else (here, there)), sems.at[k])


def through(count, step, before=None, after=None):
    def part(k, _):
        if before is not None:
            before(k)
        lax.fori_loop(k * PART, (k + 1) * PART, step, 0)
        if after is not None:
            after(k)
        return 0

    lax.fori_loop(0, count // PART, part, 0)


def each(count, act):
    def one(k, _):
        act(k)
        return 0

    lax.fori_loop(0, count, one, 0)


def first_body(mine, group, store, out, state, kept, acc, sems):
    targets = target_factor(mine[...]).astype(BF16)
    row = row_of(mine.shape[1])
    norm2 = total(jnp.where(row >= 4, group[...] * group[...], 0.0))
    size = jnp.sqrt(norm2 + TINY)
    state[...] = row_with([size, norm2 / (size * size)], 0)
    acc[...] = jnp.zeros_like(acc)

    def step(c, _):
        pts = group[c]
        twice = (SCALE * pts[3:4] / size) * jnp.where(row >= 4, pts, pltpu.roll(pts, 4, 0))
        moments = moment_block(moment_rows(pts, twice))
        kept[c] = add_chunk(acc, upright(source_factor(pts)), targets, moments, HILO_FIRST)
        return 0

    through(group.shape[0], step, after=lambda k: parcel(kept, store, sems, k, False).start())
    vel = velocity(mine[...], acc[...])
    for p in range(out.shape[0]):
        out[p] = vel
    each(group.shape[0] // PART, lambda k: parcel(kept, store, sems, k, False).wait())


def fetch(store, kept, sems):
    each(store.shape[0] // PART, lambda k: parcel(kept, store, sems, k, True).start())


def next_vector(group, state0, earlier, image, vector):
    basis = [data_rows(group[...]) / state0[0:1, 0:1]] + [q[...] for q in earlier]
    s = image[...]
    inner = [total(s * q) for q in basis]
    for b, q in zip(inner, basis):
        s = s - b * q
    norm2 = total(s * s)
    size = jnp.sqrt(norm2 + TINY)
    vector[...] = s / size
    return inner + [size, norm2 / (size * size)]


def apply_vector(mine, group, store, vector, kept, ready, acc, sems):
    chunks = group.shape[0]
    acc[...] = jnp.zeros_like(acc)

    def moments(c):
        pts = group[c]
        four = vector[c] * (SCALE * pts[3:4])
        return moment_block(moment_rows(pts, jnp.concatenate([four, four], axis=0)))

    def step(c, _):
        now = ready[c % 2]
        ready[(c + 1) % 2] = moments((c + 1) % chunks)
        acc[...] += jnp.dot(now, kept[c], preferred_element_type=F32)
        return 0

    ready[0] = moments(0)
    through(chunks, step, before=lambda k: parcel(kept, store, sems, k, True).wait())
    return velocity(mine[...], acc[...])


def second_body(mine, group, store, state0, image, after, vector, out, state, kept, ready, acc, sems):
    fetch(store, kept, sems)
    state[...] = row_with(next_vector(group, state0, [], image, vector), 2)
    vel = apply_vector(mine, group, store, vector, kept, ready, acc, sems)
    for p in range(out.shape[0]):
        out[p] = vel


def third_body(mine, group, store, state0, q1, image, after, vector, out, state, kept, ready, acc, sems):
    fetch(store, kept, sems)
    state[...] = row_with(next_vector(group, state0, [q1], image, vector), 5)
    vel = apply_vector(mine, group, store, vector, kept, ready, acc, sems)
    for p in range(out.shape[0]):
        out[p] = vel


def fourth_body(at, mine, group, store, state0, state1, state2, q1, q2, image, after, vector, basis, out, kept, ready, acc, sems):
    fetch(store, kept, sems)
    state3 = row_with(next_vector(group, state0, [q1, q2], image, vector), 9)
    vel = apply_vector(mine, group, store, vector, kept, ready, acc, sems)
    own = [mine[4:8] / state0[0:1, 0:1]] + [q[at[0]] for q in (q1, q2, vector)]
    for k, q in enumerate(own):
        basis[k] = q
    last = row_with([total(vel * q) for q in own] + [total(vel * vel)], 14)
    out[...] = jnp.broadcast_to(state0[...] + state1[...] + state2[...] + state3 + last, out.shape)


def data_rows(block):
    return block[:, 4:8, :]


def cells_body(centre, state0, own, group, q1, q2, q3, out, acc, left, ready):
    used = out.shape[3]
    width = own.shape[2]
    shift = jnp.where(row_of(width) == 0, centre[0], 0.0)
    size = state0[0:1, 0:1]
    chunks = group.shape[0]
    acc[...] = jnp.zeros_like(acc)
    for i in range(own.shape[0]):
        left[i * used : (i + 1) * used, :] = upright(target_factor(own[i] - shift))[:used]

    def moments(c):
        pts = group[c]
        area = SCALE * pts[3:4]
        groups = []
        for v in (pts[4:8] / size, q1[c], q2[c], q3[c]):
            four = area * v
            groups += moment_rows(pts, jnp.concatenate([four, four], axis=0))
        return moment_block(groups)

    def step(c, _):
        now = ready[c % 2]
        ready[(c + 1) % 2] = moments((c + 1) % chunks)
        columns = source_factor(group[c]).astype(BF16)
        values = kernel_values(jnp.dot(left[...], columns, preferred_element_type=F32), False)[0]
        acc[...] += lax.dot_general(values, now, (((1,), (1,)), ((), ())), preferred_element_type=F32)
        return 0

    ready[0] = moments(0)
    lax.fori_loop(0, chunks, step, 0)
    for i in range(own.shape[0]):
        part = acc[i * used : (i + 1) * used, :]
        full = jnp.concatenate([part, jnp.zeros((width - used, part.shape[1]), F32)], axis=0)
        full = jnp.concatenate([full, jnp.zeros((width, 256 - part.shape[1]), F32)], axis=1)
        rows = jnp.transpose(full)
        for k in range(4):
            sums = rows[16 * k : 16 * k + 16] + rows[64 + 16 * k : 80 + 16 * k] + rows[128 + 16 * k : 144 + 16 * k]
            out[k, i] = assemble(own[i] - shift, sums)[:, :used]


def krylov(local, gram, start, size):
    def dot(a, b):
        both = sum(gram[k] * x * y for k, (x, y) in enumerate(zip(a, b)))
        return jnp.broadcast_to(jnp.sum(both, axis=0, keepdims=True), both.shape)

    beta = jnp.sqrt(dot([start], [start]) + FLOOR)
    basis = [[start / beta]]
    hess = {}
    for j in range(size):
        v = basis[j]
        w = []
        for k in range(j + 2):
            part = sum(local[(k, m)] * v[m] for m in range(max(k - 1, 0), j + 1))
            w.append(0.5 * v[k] + part if k <= j else part)
        for i in range(j + 1):
            h = dot(w, basis[i])
            hess[(i, j)] = h
            w = [x - h * basis[i][k] if k <= i else x for k, x in enumerate(w)]
        h = jnp.sqrt(dot(w, w) + FLOOR)
        hess[(j + 1, j)] = h
        inverse = 1.0 / h
        basis.append([x * inverse for x in w])
    y = solve_small(hess, beta, size)
    return [sum(y[j] * basis[j][k] for j in range(k, size)) for k in range(size)]


def last_body(at, red, basis, near0, near1, near2, wall, velocity_out, density_out):
    segments = 8
    peers = red.shape[0] // segments
    rows = [jnp.sum(red[s * peers : (s + 1) * peers, :], axis=0, keepdims=True) for s in range(segments)]
    table = jnp.concatenate(rows, axis=0)
    column = lambda k: jnp.broadcast_to(table[:, k : k + 1], (segments, 128))
    same = lambda k: column(k) * (1.0 / peers)
    local, gram = {}, [same(1)]
    start = same(0)
    for m, first in ((0, 2), (1, 5), (2, 9)):
        for k in range(m + 2):
            local[(k, m)] = same(first + k)
        gram.append(same(first + m + 2))
    norm2 = column(18)
    for k in range(4):
        inner = column(14 + k)
        local[(k, 3)] = inner
        norm2 = norm2 - inner * inner * (2.0 - gram[k])
    norm2 = jnp.maximum(norm2, 0.0)
    size = jnp.sqrt(norm2 + TINY)
    local[(4, 3)] = size
    gram.append(norm2 / (size * size))
    coords = krylov(local, gram, start, 4)
    mine = lax.broadcasted_iota(jnp.int32, (segments, 128), 0) == at[0]
    z = [jnp.sum(jnp.where(mine, x, 0.0), axis=0, keepdims=True) for x in coords]
    points = basis.shape[2]
    wide = [jnp.concatenate([x] * (points // 128), axis=1) for x in z]
    density = wide[0] * basis[0]
    for k in range(1, 4):
        density = density + wide[k] * basis[k]
    density_out[...] = density[0:3]
    for i in range(near0.shape[0]):
        part = near0[i] + near1[i] + near2[i]
        for k in range(4):
            part = part + wide[k][:, : part.shape[1]] * wall[k, i]
        velocity_out[:, i, :] = part[0:3]


HILO_FIRST = False
HILO = False
TINY = 1e-30
THREE = 3
PART = 2


def swap(x, axes):
    return lax.all_to_all(x, axes, 0, 0, tiled=True)


def per_device(cell_points, cell_force, cell_weight, partners, wall_points, wall_area, wall_data):
    cells, _, surface = cell_points.shape
    points = wall_points.shape[1]
    segments, peers = lax.axis_size("wall"), lax.axis_size("cell")
    width = -(-surface // 128) * 128
    segment = lax.axis_index("wall")
    centre = 8.0 * segment.astype(F32) + 4.0
    at = lax.axis_index("cell").astype(jnp.int32)[None]

    copies = shape(peers, 4, points)
    row = shape(1, 128)
    given = (
        wall_points,
        wall_area.reshape(points // 128, 128),
        wall_data,
        jnp.transpose(cell_points, (1, 0, 2)),
        jnp.transpose(cell_force, (1, 0, 2)),
        cell_weight,
    )
    mine, own, sent_wall, sent_cells = call(
        pack_body,
        [shape(8, points), shape(cells, 8, width), shape(peers, 8, points), shape(peers, cells, 8, width)],
        (centre[None], *(pltpu.with_memory_space_constraint(x, pltpu.HBM) for x in given)),
        "pack",
        [pltpu.VMEM(x.shape, F32) for x in given] + [pltpu.SemaphoreType.DMA((len(given),))],
        smem=(0,),
        apart=range(1, 1 + len(given)),
    )
    group = swap(sent_wall, "cell")
    everyone = swap(sent_cells, "cell")
    scratch = (
        pltpu.VMEM((peers, points, points), BF16),
        pltpu.VMEM((48, points), F32),
        pltpu.SemaphoreType.DMA((peers // PART,)),
    )
    later = (scratch[0], pltpu.VMEM((2, 48, points), BF16), *scratch[1:])

    def near(k):
        return call(
            lambda *refs: near_body(THREE * k, *refs),
            [shape(cells, 4, surface)],
            (partners, own, everyone),
            "near" + str(k),
            (pltpu.VMEM((8, THREE * width), F32), pltpu.VMEM((48, surface), F32)),
            smem=(0,),
        )[0]

    store, s0, state0 = call(
        first_body,
        [shape(peers, points, points, dtype=BF16), copies, row],
        (mine, group),
        "first",
        scratch,
        apart_out=(0,),
    )
    near0 = near(0)
    q1, s1, state1 = call(
        second_body,
        [copies, copies, row],
        (mine, group, store, state0, swap(s0, "cell"), near0),
        "second",
        later,
        apart=(2, 5),
    )
    near1 = near(1)
    q2, s2, state2 = call(
        third_body,
        [copies, copies, row],
        (mine, group, store, state0, q1, swap(s1, "cell"), near1),
        "third",
        later,
        apart=(2, 6),
    )
    near2 = near(2)
    q3, basis, sums = call(
        fourth_body,
        [copies, shape(4, 4, points), shape(segments * peers, 128)],
        (at, mine, group, store, state0, state1, state2, q1, q2, swap(s2, "cell"), near2),
        "fourth",
        later,
        smem=(0,),
        apart=(3, 10),
    )
    red = swap(sums, AXES)
    (wall,) = call(
        cells_body,
        [shape(4, cells, 4, surface)],
        (centre[None], state0, own, group, q1, q2, q3),
        "cells",
        (
            pltpu.VMEM((cells * surface, 192), F32),
            pltpu.VMEM((cells * surface, 48), BF16),
            pltpu.VMEM((2, 192, points), BF16),
        ),
        smem=(0,),
    )
    velocity_out, density = call(
        last_body,
        [shape(3, cells, surface), shape(3, points)],
        (segment.astype(jnp.int32)[None], red, basis, near0, near1, near2, wall),
        "last",
        smem=(0,),
    )
    return jnp.transpose(velocity_out, (1, 0, 2)), density


def solution(mesh):
    in_specs = (
        P(AXES, None, None),
        P(AXES, None, None),
        P(AXES, None),
        P(AXES, None),
        P(None, AXES),
        P(AXES),
        P(None, AXES),
    )
    out_specs = (P(AXES, None, None), P(None, AXES))
    step = jax.shard_map(per_device, mesh=mesh, in_specs=in_specs, out_specs=out_specs, check_vma=False)
    return step
```

```python
import math

import jax
import jax.numpy as jnp
from jax import lax
from jax.experimental import pallas as pl
from jax.experimental.pallas import tpu as pltpu
from jax.sharding import PartitionSpec as P

F32 = jnp.float32
BF16 = jnp.bfloat16
AXES = ("wall", "cell")
E2 = 0.1 * 0.1
FLOOR = 1e-06
SCALE = 1.0 / (8.0 * math.pi)
VMEM_LIMIT = 48 * 2**20


def row_of(n):
    return lax.broadcasted_iota(jnp.int32, (8, n), 0)


def split3(a):
    high = a.astype(BF16).astype(F32)
    rest = a - high
    mid = rest.astype(BF16).astype(F32)
    low = (rest - mid).astype(BF16).astype(F32)
    return high, mid, low


def target_factor(points):
    row = row_of(points.shape[1])
    coords = jnp.where(row < 3, points, 0.0)
    norm2 = jnp.sum(coords * coords, axis=0, keepdims=True) + E2
    eight = jnp.where(row < 3, -2.0 * coords, jnp.where(row == 3, 1.0, jnp.where(row == 4, norm2, 0.0)))
    h, m, l = split3(eight)
    return jnp.concatenate([h, m, l, h, m, h], axis=0)


def source_factor(points):
    row = row_of(points.shape[1])
    coords = jnp.where(row < 3, points, 0.0)
    norm2 = jnp.sum(coords * coords, axis=0, keepdims=True)
    eight = jnp.where(row < 3, coords, jnp.where(row == 3, norm2, jnp.where(row == 4, 1.0, 0.0)))
    h, m, l = split3(eight)
    return jnp.concatenate([h, h, h, m, m, l], axis=0)


def upright(a):
    wide = jnp.concatenate([a, jnp.zeros((128 - a.shape[0], a.shape[1]), F32)], axis=0)
    return jnp.transpose(wide)[:, : a.shape[0]].astype(BF16)


def moment_rows(points, twice):
    row = row_of(points.shape[1])
    coords = jnp.where(row < 3, points, 0.0)
    y0, y1, y2 = points[0:1], points[1:2], points[2:3]
    norm2 = jnp.sum(coords * coords, axis=0, keepdims=True)
    inner = jnp.sum(coords * twice, axis=0, keepdims=True)
    e = norm2 * twice + inner * coords
    first = twice * jnp.where(row < 4, 1.0, y0)
    first = jnp.where(row == 3, e[0:1], jnp.where(row == 7, e[1:2], first))
    second = twice * jnp.where(row < 4, y1, y2)
    second = jnp.where(row == 3, e[2:3], second)
    return [first, second]


def moment_block(groups):
    parts = [split3(g) for g in groups]
    return jnp.concatenate([p[k] for k in range(3) for p in parts], axis=0).astype(BF16)


def kernel_values(shifted, hilo):
    inv = lax.rsqrt(shifted)
    kern = inv * inv * inv
    high = kern.astype(BF16)
    return [high, (kern - high.astype(F32)).astype(BF16)] if hilo else [high]


def add_chunk(acc, sources, targets, moments, hilo):
    parts = kernel_values(jnp.dot(sources, targets, preferred_element_type=F32), hilo)
    acc[...] += jnp.dot(moments, parts[0], preferred_element_type=F32)
    if hilo:
        acc[0:32, :] += jnp.dot(moments[0:32], parts[1], preferred_element_type=F32)
    return parts[0]


def assemble(points, rows):
    f, t0, t1, t2 = rows[0:4], rows[4:8], rows[8:12], rows[12:16]
    n = points.shape[1]
    row = lax.broadcasted_iota(jnp.int32, (4, n), 0)
    x4 = jnp.where(row < 3, points[0:4], 0.0)
    x0, x1, x2 = x4[0:1], x4[1:2], x4[2:3]
    norm2 = jnp.sum(x4 * x4, axis=0, keepdims=True)
    along = jnp.sum(x4 * f, axis=0, keepdims=True) - (t0[0:1] + t1[1:2] + t2[2:3])
    s0 = jnp.sum(x4 * t0, axis=0, keepdims=True)
    s1 = jnp.sum(x4 * t1, axis=0, keepdims=True)
    s2 = jnp.sum(x4 * t2, axis=0, keepdims=True)
    e = jnp.where(row == 0, f[3:4] - s0, jnp.where(row == 1, t0[3:4] - s1, t1[3:4] - s2))
    return jnp.where(row < 3, (norm2 + 2.0 * E2) * f + e - 2.0 * (x0 * t0 + x1 * t1 + x2 * t2) + x4 * along, 0.0)


def velocity(points, acc):
    return assemble(points, acc[0:16] + acc[16:32] + acc[32:48])


def solve_small(hess, beta, size):
    zero = jnp.zeros_like(beta)
    upper = [[hess.get((r, c), zero) for c in range(size)] for r in range(size + 1)]
    targets = [beta] + [zero] * size
    cosines, sines = [], []
    for column in range(size):
        for prior in range(column):
            a, b = upper[prior][column], upper[prior + 1][column]
            upper[prior][column] = cosines[prior] * a + sines[prior] * b
            upper[prior + 1][column] = cosines[prior] * b - sines[prior] * a
        a, b = upper[column][column], upper[column + 1][column]
        radius = jnp.sqrt(a * a + b * b)
        cosines.append(a / radius)
        sines.append(b / radius)
        upper[column][column] = radius
        targets[column + 1] = -sines[column] * targets[column]
        targets[column] = cosines[column] * targets[column]
    weights = [None] * size
    for column in reversed(range(size)):
        part = targets[column]
        for later in range(column + 1, size):
            part = part - upper[column][later] * weights[later]
        weights[column] = part / upper[column][column]
    return weights


def row_with(values, start):
    lane = lax.broadcasted_iota(jnp.int32, (1, 128), 1)
    row = jnp.zeros((1, 128), F32)
    for k, v in enumerate(values):
        row = jnp.where(lane == start + k, jnp.broadcast_to(v, (1, 128)), row)
    return row


def total(a):
    while a.ndim > 2:
        a = jnp.sum(a, axis=0)
    return jnp.sum(jnp.sum(a, axis=0, keepdims=True), axis=1, keepdims=True)


def call(body, outs, ins, name, scratch=(), smem=(), apart=(), apart_out=()):
    def whole(dims):
        return pl.BlockSpec(dims, lambda i: (0,) * len(dims))

    in_specs = []
    for k, x in enumerate(ins):
        if k in smem:
            in_specs.append(pl.BlockSpec(memory_space=pltpu.SMEM))
        elif k in apart:
            in_specs.append(pl.BlockSpec(memory_space=pltpu.HBM))
        else:
            in_specs.append(whole(x.shape))
    out_specs = [
        pl.BlockSpec(memory_space=pltpu.HBM) if k in apart_out else whole(x.shape) for k, x in enumerate(outs)
    ]
    return pl.pallas_call(
        body,
        grid=(1,),
        out_shape=outs,
        in_specs=in_specs,
        out_specs=out_specs,
        scratch_shapes=list(scratch),
        compiler_params=pltpu.CompilerParams(vmem_limit_bytes=VMEM_LIMIT),
        name=name,
    )(*ins)


def shape(*dims, dtype=F32):
    return jax.ShapeDtypeStruct(dims, dtype)


def held(body, count):
    def kernel(*refs):
        given, rest, copies, sems = refs[:count], refs[count : -count - 1], refs[-count - 1 : -1], refs[-1]
        moves = [pltpu.make_async_copy(x, y, sems.at[k]) for k, (x, y) in enumerate(zip(given, copies))]
        for m in moves:
            m.start()
        for m in moves:
            m.wait()
        body(*copies, *rest)

    return kernel


def pack_wall_body(points, area, data, centre, mine, sent):
    n = points.shape[1]
    row = lax.broadcasted_iota(jnp.int32, (3, n), 0)
    mine[0:3] = points[...] - jnp.where(row == 0, centre[0], 0.0)
    mine[3:4] = jnp.concatenate([area[k : k + 1] for k in range(area.shape[0])], axis=1)
    mine[4:7] = data[...]
    mine[7:8] = jnp.zeros((1, n), F32)
    for p in range(sent.shape[0]):
        sent[p] = mine[...]


def pack_cells_body(cell_points, cell_force, cell_weight, own, sent):
    used = cell_points.shape[2]
    own[...] = jnp.zeros_like(own)
    for i in range(own.shape[0]):
        own[i, 0:3, 0:used] = cell_points[:, i, :]
        own[i, 4:7, 0:used] = cell_force[:, i, :] * cell_weight[i : i + 1, :]
    for p in range(sent.shape[0]):
        sent[p] = own[...]


def near_body(first, partners, own, everyone, out, sources, acc):
    cells = own.shape[0]
    width = own.shape[2]
    used = out.shape[2]
    row = row_of(width)
    r = row_of(THREE * width)
    for i in range(cells):
        mine = own[i]
        centre = jnp.where(row < 3, mine[:, 0:1], 0.0)
        for k in range(THREE):
            slot = first + k
            if slot == 0:
                sources[:, 0:width] = mine - centre
                continue
            n = partners[i, slot - 1]
            there = jnp.maximum(n, 0)
            other = everyone[there // cells, there % cells] - centre
            keep = jnp.where(n >= 0, 1.0, 0.0)
            sources[:, k * width : (k + 1) * width] = jnp.where(row >= 4, other * keep, other)
        targets = target_factor(mine - centre).astype(BF16)[:, :used]
        pts = sources[...]
        twice = SCALE * jnp.where(r >= 4, pts, pltpu.roll(pts, 4, 0))
        acc[...] = jnp.zeros_like(acc)
        add_chunk(acc, upright(source_factor(pts)), targets, moment_block(moment_rows(pts, twice)), True)
        out[i] = velocity((mine - centre)[:, :used], acc[...])


def parcel(near, far, sems, k, inward):
    here, there = near.at[pl.ds(k * PART, PART)], far.at[pl.ds(k * PART, PART)]
    return pltpu.make_async_copy(*((there, here) if inward else (here, there)), sems.at[k])


def through(count, step, before=None, after=None):
    def part(k, _):
        if before is not None:
            before(k)
        lax.fori_loop(k * PART, (k + 1) * PART, step, 0)
        if after is not None:
            after(k)
        return 0

    lax.fori_loop(0, count // PART, part, 0)


def each(count, act):
    def one(k, _):
        act(k)
        return 0

    lax.fori_loop(0, count, one, 0)


def first_body(mine, group, store, out, state, kept, acc, sems):
    targets = target_factor(mine[...]).astype(BF16)
    row = row_of(mine.shape[1])
    norm2 = total(jnp.where(row >= 4, group[...] * group[...], 0.0))
    size = jnp.sqrt(norm2 + TINY)
    state[...] = row_with([size, norm2 / (size * size)], 0)
    acc[...] = jnp.zeros_like(acc)

    def step(c, _):
        pts = group[c]
        twice = (SCALE * pts[3:4] / size) * jnp.where(row >= 4, pts, pltpu.roll(pts, 4, 0))
        moments = moment_block(moment_rows(pts, twice))
        kept[c] = add_chunk(acc, upright(source_factor(pts)), targets, moments, HILO_FIRST)
        return 0

    count = store.shape[0]
    through(count, step, after=lambda k: parcel(kept, store, sems, k, False).start())
    lax.fori_loop(count, group.shape[0], step, 0)
    vel = velocity(mine[...], acc[...])
    for p in range(out.shape[0]):
        out[p] = vel
    each(count // PART, lambda k: parcel(kept, store, sems, k, False).wait())


def fetch(store, kept, sems):
    each(store.shape[0] // PART, lambda k: parcel(kept, store, sems, k, True).start())


def next_vector(group, state0, earlier, image, vector):
    basis = [data_rows(group[...]) / state0[0:1, 0:1]] + [q[...] for q in earlier]
    s = image[...]
    inner = [total(s * q) for q in basis]
    for b, q in zip(inner, basis):
        s = s - b * q
    norm2 = total(s * s)
    size = jnp.sqrt(norm2 + TINY)
    vector[...] = s / size
    return inner + [size, norm2 / (size * size)]


def apply_vector(mine, group, store, vector, kept, ready, acc, sems):
    chunks = group.shape[0]
    acc[...] = jnp.zeros_like(acc)

    def moments(c):
        pts = group[c]
        four = vector[c] * (SCALE * pts[3:4])
        return moment_block(moment_rows(pts, jnp.concatenate([four, four], axis=0)))

    def step(c, _):
        now = ready[c % 2]
        ready[(c + 1) % 2] = moments((c + 1) % chunks)
        acc[...] += jnp.dot(now, kept[c], preferred_element_type=F32)
        return 0

    def again(c, _):
        now = ready[c % 2]
        ready[(c + 1) % 2] = moments((c + 1) % chunks)
        add_chunk(acc, upright(source_factor(group[c])), targets, now, False)
        return 0

    count = store.shape[0]
    targets = target_factor(mine[...]).astype(BF16)
    ready[count % 2] = moments(count)
    lax.fori_loop(count, chunks, again, 0)
    through(count, step, before=lambda k: parcel(kept, store, sems, k, True).wait())
    return velocity(mine[...], acc[...])


def second_body(mine, group, store, state0, image, after, vector, out, state, kept, ready, acc, sems):
    fetch(store, kept, sems)
    state[...] = row_with(next_vector(group, state0, [], image, vector), 2)
    vel = apply_vector(mine, group, store, vector, kept, ready, acc, sems)
    for p in range(out.shape[0]):
        out[p] = vel


def third_body(mine, group, store, state0, q1, image, after, vector, out, state, kept, ready, acc, sems):
    fetch(store, kept, sems)
    state[...] = row_with(next_vector(group, state0, [q1], image, vector), 5)
    vel = apply_vector(mine, group, store, vector, kept, ready, acc, sems)
    for p in range(out.shape[0]):
        out[p] = vel


def fourth_body(at, mine, group, store, state0, state1, state2, q1, q2, image, after, vector, basis, out, kept, ready, acc, sems):
    fetch(store, kept, sems)
    state3 = row_with(next_vector(group, state0, [q1, q2], image, vector), 9)
    vel = apply_vector(mine, group, store, vector, kept, ready, acc, sems)
    own = [mine[4:8] / state0[0:1, 0:1]] + [q[at[0]] for q in (q1, q2, vector)]
    for k, q in enumerate(own):
        basis[k] = q
    last = row_with([total(vel * q) for q in own] + [total(vel * vel)], 14)
    out[...] = jnp.broadcast_to(state0[...] + state1[...] + state2[...] + state3 + last, out.shape)


def data_rows(block):
    return block[:, 4:8, :]


def cells_body(centre, state0, own, group, q1, q2, q3, out, acc, left, ready):
    used = out.shape[3]
    width = own.shape[2]
    shift = jnp.where(row_of(width) == 0, centre[0], 0.0)
    size = state0[0:1, 0:1]
    chunks = group.shape[0]
    acc[...] = jnp.zeros_like(acc)
    for i in range(own.shape[0]):
        left[i * used : (i + 1) * used, :] = upright(target_factor(own[i] - shift))[:used]

    def moments(c):
        pts = group[c]
        area = SCALE * pts[3:4]
        groups = []
        for v in (pts[4:8] / size, q1[c], q2[c], q3[c]):
            four = area * v
            groups += moment_rows(pts, jnp.concatenate([four, four], axis=0))
        return moment_block(groups)

    def step(c, _):
        now = ready[c % 2]
        ready[(c + 1) % 2] = moments((c + 1) % chunks)
        columns = source_factor(group[c]).astype(BF16)
        values = kernel_values(jnp.dot(left[...], columns, preferred_element_type=F32), False)[0]
        acc[...] += lax.dot_general(values, now, (((1,), (1,)), ((), ())), preferred_element_type=F32)
        return 0

    ready[0] = moments(0)
    lax.fori_loop(0, chunks, step, 0)
    for i in range(own.shape[0]):
        part = acc[i * used : (i + 1) * used, :]
        full = jnp.concatenate([part, jnp.zeros((width - used, part.shape[1]), F32)], axis=0)
        full = jnp.concatenate([full, jnp.zeros((width, 256 - part.shape[1]), F32)], axis=1)
        rows = jnp.transpose(full)
        for k in range(4):
            sums = rows[16 * k : 16 * k + 16] + rows[64 + 16 * k : 80 + 16 * k] + rows[128 + 16 * k : 144 + 16 * k]
            out[k, i] = assemble(own[i] - shift, sums)[:, :used]


def krylov(local, gram, start, size):
    def dot(a, b):
        both = sum(gram[k] * x * y for k, (x, y) in enumerate(zip(a, b)))
        return jnp.broadcast_to(jnp.sum(both, axis=0, keepdims=True), both.shape)

    beta = jnp.sqrt(dot([start], [start]) + FLOOR)
    basis = [[start / beta]]
    hess = {}
    for j in range(size):
        v = basis[j]
        w = []
        for k in range(j + 2):
            part = sum(local[(k, m)] * v[m] for m in range(max(k - 1, 0), j + 1))
            w.append(0.5 * v[k] + part if k <= j else part)
        for i in range(j + 1):
            h = dot(w, basis[i])
            hess[(i, j)] = h
            w = [x - h * basis[i][k] if k <= i else x for k, x in enumerate(w)]
        h = jnp.sqrt(dot(w, w) + FLOOR)
        hess[(j + 1, j)] = h
        inverse = 1.0 / h
        basis.append([x * inverse for x in w])
    y = solve_small(hess, beta, size)
    return [sum(y[j] * basis[j][k] for j in range(k, size)) for k in range(size)]


def last_body(at, red, basis, near0, near1, near2, wall, velocity_out, density_out):
    segments = 8
    peers = red.shape[0] // segments
    rows = [jnp.sum(red[s * peers : (s + 1) * peers, :], axis=0, keepdims=True) for s in range(segments)]
    table = jnp.concatenate(rows, axis=0)
    column = lambda k: jnp.broadcast_to(table[:, k : k + 1], (segments, 128))
    same = lambda k: column(k) * (1.0 / peers)
    local, gram = {}, [same(1)]
    start = same(0)
    for m, first in ((0, 2), (1, 5), (2, 9)):
        for k in range(m + 2):
            local[(k, m)] = same(first + k)
        gram.append(same(first + m + 2))
    norm2 = column(18)
    for k in range(4):
        inner = column(14 + k)
        local[(k, 3)] = inner
        norm2 = norm2 - inner * inner * (2.0 - gram[k])
    norm2 = jnp.maximum(norm2, 0.0)
    size = jnp.sqrt(norm2 + TINY)
    local[(4, 3)] = size
    gram.append(norm2 / (size * size))
    coords = krylov(local, gram, start, 4)
    mine = lax.broadcasted_iota(jnp.int32, (segments, 128), 0) == at[0]
    z = [jnp.sum(jnp.where(mine, x, 0.0), axis=0, keepdims=True) for x in coords]
    points = basis.shape[2]
    wide = [jnp.concatenate([x] * (points // 128), axis=1) for x in z]
    density = wide[0] * basis[0]
    for k in range(1, 4):
        density = density + wide[k] * basis[k]
    density_out[...] = density[0:3]
    for i in range(near0.shape[0]):
        part = near0[i] + near1[i] + near2[i]
        for k in range(4):
            part = part + wide[k][:, : part.shape[1]] * wall[k, i]
        velocity_out[:, i, :] = part[0:3]


HILO_FIRST = False
HILO = False
TINY = 1e-30
THREE = 3
PART = 2
AGAIN = 2


def swap(x, axes):
    return lax.all_to_all(x, axes, 0, 0, tiled=True)


def per_device(cell_points, cell_force, cell_weight, partners, wall_points, wall_area, wall_data):
    cells, _, surface = cell_points.shape
    points = wall_points.shape[1]
    segments, peers = lax.axis_size("wall"), lax.axis_size("cell")
    width = -(-surface // 128) * 128
    segment = lax.axis_index("wall")
    centre = 8.0 * segment.astype(F32) + 4.0
    at = lax.axis_index("cell").astype(jnp.int32)[None]

    copies = shape(peers, 4, points)
    row = shape(1, 128)
    def pack(body, outs, given, more, name):
        given = [pltpu.with_memory_space_constraint(x, pltpu.HBM) for x in given]
        return call(
            held(body, 3),
            outs,
            (*given, *more),
            name,
            [pltpu.VMEM(x.shape, F32) for x in given] + [pltpu.SemaphoreType.DMA((3,))],
            smem=(3,),
            apart=(0, 1, 2),
        )

    mine, sent_wall = pack(
        pack_wall_body,
        [shape(8, points), shape(peers, 8, points)],
        (wall_points, wall_area.reshape(points // 128, 128), wall_data),
        (centre[None],),
        "pack_wall",
    )
    own, sent_cells = pack(
        pack_cells_body,
        [shape(cells, 8, width), shape(peers, cells, 8, width)],
        (jnp.transpose(cell_points, (1, 0, 2)), jnp.transpose(cell_force, (1, 0, 2)), cell_weight),
        (),
        "pack_cells",
    )
    group = swap(sent_wall, "cell")
    everyone = swap(sent_cells, "cell")
    scratch = (
        pltpu.VMEM((peers, points, points), BF16),
        pltpu.VMEM((48, points), F32),
        pltpu.SemaphoreType.DMA((peers // PART,)),
    )
    later = (pltpu.VMEM((peers - AGAIN, points, points), BF16), pltpu.VMEM((2, 48, points), BF16), *scratch[1:])

    def near(k):
        return call(
            lambda *refs: near_body(THREE * k, *refs),
            [shape(cells, 4, surface)],
            (partners, own, everyone),
            "near" + str(k),
            (pltpu.VMEM((8, THREE * width), F32), pltpu.VMEM((48, surface), F32)),
            smem=(0,),
        )[0]

    store, s0, state0 = call(
        first_body,
        [shape(peers - AGAIN, points, points, dtype=BF16), copies, row],
        (mine, group),
        "first",
        scratch,
        apart_out=(0,),
    )
    near0 = near(0)
    q1, s1, state1 = call(
        second_body,
        [copies, copies, row],
        (mine, group, store, state0, swap(s0, "cell"), near0),
        "second",
        later,
        apart=(2, 5),
    )
    near1 = near(1)
    q2, s2, state2 = call(
        third_body,
        [copies, copies, row],
        (mine, group, store, state0, q1, swap(s1, "cell"), near1),
        "third",
        later,
        apart=(2, 6),
    )
    near2 = near(2)
    q3, basis, sums = call(
        fourth_body,
        [copies, shape(4, 4, points), shape(segments * peers, 128)],
        (at, mine, group, store, state0, state1, state2, q1, q2, swap(s2, "cell"), near2),
        "fourth",
        later,
        smem=(0,),
        apart=(3, 10),
    )
    red = swap(sums, AXES)
    (wall,) = call(
        cells_body,
        [shape(4, cells, 4, surface)],
        (centre[None], state0, own, group, q1, q2, q3),
        "cells",
        (
            pltpu.VMEM((cells * surface, 192), F32),
            pltpu.VMEM((cells * surface, 48), BF16),
            pltpu.VMEM((2, 192, points), BF16),
        ),
        smem=(0,),
    )
    velocity_out, density = call(
        last_body,
        [shape(3, cells, surface), shape(3, points)],
        (segment.astype(jnp.int32)[None], red, basis, near0, near1, near2, wall),
        "last",
        smem=(0,),
    )
    return jnp.transpose(velocity_out, (1, 0, 2)), density


def solution(mesh):
    in_specs = (
        P(AXES, None, None),
        P(AXES, None, None),
        P(AXES, None),
        P(AXES, None),
        P(None, AXES),
        P(AXES),
        P(None, AXES),
    )
    out_specs = (P(AXES, None, None), P(None, AXES))
    step = jax.shard_map(per_device, mesh=mesh, in_specs=in_specs, out_specs=out_specs, check_vma=False)
    return step
```
